32 devices in a mesh: space: 16 (over z, x, core), chan: 2 (over y).
Axes of the slice: x: 2, y: 2, z: 4, core: 2. Of those that a mesh axis runs over, the one named last changes fastest.
Arguments:
- patches: bfloat16 [16, 4096, 1024], P('chan', 'space'), may hold values from -6 to 6
- var_embed: float32 [16, 1024], P('chan'), may hold values from -3 to 3
- agg_query: float32 [1024], replicated, may hold values from -18 to 18
- pos_embed: bfloat16 [4096, 1024], P('space'), may hold values from -3 to 3
- gain_first: float32 [1024], replicated, may hold values from 0.1 to 1.9
- gain_second: float32 [1024], replicated, may hold values from 0.1 to 1.9
- w_qkv: bfloat16 [1024, 3, 1024], P(None, None, 'chan'), may hold values from -0.3 to 0.3
- w_out: bfloat16 [1024, 1024], P('chan'), may hold values from -0.1875 to 0.1875
- w_dec: bfloat16 [1024, 1024], replicated, may hold values from -0.1875 to 0.1875
- mod_scale: float32 [16, 1024], P('chan'), may hold values from -3 to 3
- mod_shift: float32 [16, 1024], P('chan'), may hold values from -3 to 3
Outputs:
- decoded: bfloat16 [16, 4096, 1024], P('chan', 'space')
The draws below stay inside these ranges and needn't reach their ends.
All inputs are finite; a program needn't handle non-finite values.
Results may differ from the reference program's by a relative error of at most 0.025.
Values may be sent and summed in bfloat16 or wider, within the bound.
A program may use at most 64 MiB of HBM per device.

```python
import math
import jax
import jax.numpy as jnp
from jax import lax

D = 1024
HEADS = 16
VARS = 16
POSITIONS = 4096


weight_bound = 0.296875


def query_vector(key):
    base = jax.random.normal(jax.random.fold_in(key, 11), (D,), jnp.float32)
    return jnp.clip(3.0 * base, -18.0, 18.0)


def variable_rows(key):
    base = jax.random.normal(jax.random.fold_in(key, 12), (VARS, D), jnp.float32)
    return jnp.clip(0.5 * base, -3.0, 3.0)


def draw_agg_query(key, part):
    return query_vector(key)


def draw_var_embed(key, part):
    return variable_rows(key)


def draw_patches(key, part):
    noise = jnp.clip(jax.random.normal(jax.random.fold_in(key, 13), (VARS, POSITIONS, D), jnp.float32), -6.0, 6.0)
    return noise.astype(jnp.bfloat16)


def draw_w_qkv(key, part):
    scale = 1.5 / math.sqrt(D)
    base = jnp.clip(jax.random.normal(jax.random.fold_in(key, 15), (D, 3, D), jnp.float32), -6.0, 6.0) * scale
    base = jnp.clip(base, -weight_bound, weight_bound)
    return base.astype(jnp.bfloat16)


def steps_of(stream_key, extent, pieces, least, largest):
    def one(position, blocks):
        steps = jax.random.uniform(jax.random.fold_in(jax.random.fold_in(stream_key, 6), position), (blocks,), jnp.float32, least / len(pieces), largest / len(pieces))
        return jnp.repeat(jnp.exp(steps), extent[position] // blocks).reshape((-1,) + (1,) * (len(extent) - position - 1))

    loudness = one(*pieces[0])
    for cut in pieces[1:]:
        loudness = loudness * one(*cut)
    return loudness


def centred(rng, shape, scale, limit, shards=(), dtype=jnp.bfloat16):
    drawn = jax.random.normal(rng, shape, jnp.float32) * scale
    if len(shards) > 0:
        drawn = steps_of(rng, shape, shards, -0.22, 0.18) * drawn
    return jnp.clip(drawn, min=-limit, max=limit).astype(dtype)


def setup_inputs(seed: int = 0) -> dict:
    arg_keys = jax.random.split(jax.random.key(seed), 12)
    patches = draw_patches(jax.random.fold_in(arg_keys[11], 71), 0)
    var_embed = draw_var_embed(jax.random.fold_in(arg_keys[11], 71), 0)
    agg_query = draw_agg_query(jax.random.fold_in(arg_keys[11], 71), 0)
    pos_embed = centred(arg_keys[3], (POSITIONS, D), 0.5, 3.0, ((0, 16),))
    gain_first = jnp.clip(1.0 + 0.18 * jax.random.normal(arg_keys[4], (D,), jnp.float32), 0.1, 1.9)
    gain_second = jnp.clip(1.0 + 0.18 * jax.random.normal(arg_keys[5], (D,), jnp.float32), 0.1, 1.9)
    w_qkv = draw_w_qkv(jax.random.fold_in(arg_keys[11], 71), 0)
    w_out = centred(arg_keys[7], (D, D), D ** -0.5, 0.1875, ((0, 2),))
    w_dec = centred(arg_keys[8], (D, D), D ** -0.5, 0.1875)
    mod_scale = centred(arg_keys[9], (VARS, D), 0.5, 3.0, ((0, 2),), jnp.float32)
    mod_shift = centred(arg_keys[10], (VARS, D), 0.5, 3.0, ((0, 2),), jnp.float32)
    return dict(patches=patches, var_embed=var_embed, agg_query=agg_query, pos_embed=pos_embed, gain_first=gain_first, gain_second=gain_second, w_qkv=w_qkv, w_out=w_out, w_dec=w_dec, mod_scale=mod_scale, mod_shift=mod_shift)


epsilon = 1e-06

def rms_norm(values, gain_vec):
    return values * lax.rsqrt(lax.optimization_barrier(jnp.mean(values * values, -1, keepdims=True)) + epsilon) * gain_vec

def reference(patches, var_embed, agg_query, pos_embed, gain_first, gain_second, w_qkv, w_out, w_dec, mod_scale, mod_shift):
    agg_scale = 1.0 / math.sqrt(D)

    def var_logit(pair_in):
        tokens_var, embed_var = pair_in
        embedded = tokens_var.astype(jnp.float32) + embed_var
        return lax.optimization_barrier(jnp.sum(embedded * agg_query, -1)) * agg_scale
    logits = lax.map(var_logit, (patches, var_embed))
    agg_weights = jax.nn.softmax(logits, axis=0)

    def add_var(running, triple_in):
        tokens_var, embed_var, weight_var = triple_in
        embedded = tokens_var.astype(jnp.float32) + embed_var
        return (running + weight_var[:, None] * embedded, None)
    pooled, _ = lax.scan(add_var, jnp.zeros((POSITIONS, D), jnp.float32), (patches, var_embed, agg_weights))
    resid = pooled + pos_embed.astype(jnp.float32)
    normed = rms_norm(resid, gain_first).astype(jnp.bfloat16)
    qkv_all = jnp.dot(normed, w_qkv.reshape(D, 3 * D), preferred_element_type=jnp.float32).astype(jnp.bfloat16)
    head_dim = D // HEADS
    queries = qkv_all[:, :D].reshape(POSITIONS, HEADS, head_dim).transpose(1, 0, 2)
    keys_all = qkv_all[:, D:2 * D].reshape(POSITIONS, HEADS, head_dim).transpose(1, 0, 2)
    values_all = qkv_all[:, 2 * D:].reshape(POSITIONS, HEADS, head_dim).transpose(1, 0, 2)
    inv_scale = 1.0 / math.sqrt(head_dim)

    def one_head(triple_in):
        query_head, key_head, value_head = triple_in
        scores = jnp.dot(query_head, key_head.T, preferred_element_type=jnp.float32) * inv_scale
        probs = jax.nn.softmax(scores, axis=-1).astype(jnp.bfloat16)
        return jnp.dot(probs, value_head, preferred_element_type=jnp.float32).astype(jnp.bfloat16)
    mixed = lax.map(one_head, (queries, keys_all, values_all)).transpose(1, 0, 2).reshape(POSITIONS, D)
    trunk = resid + jnp.dot(mixed, w_out, preferred_element_type=jnp.float32)
    normed_two = rms_norm(trunk, gain_second).astype(jnp.bfloat16)

    def decode_var(pair_in):
        scale_var, shift_var = pair_in
        modulated = (normed_two.astype(jnp.float32) * (1.0 + scale_var) + shift_var).astype(jnp.bfloat16)
        return jnp.dot(modulated, w_dec, preferred_element_type=jnp.float32).astype(jnp.bfloat16)
    return lax.map(decode_var, (mod_scale, mod_shift))
```

```python
import functools
import math

import jax
import jax.numpy as jnp
from jax import lax
from jax.experimental import pallas as pl
from jax.experimental.pallas import tpu as pltpu
from jax.sharding import PartitionSpec as P

D = 1024
HEADS = 16


epsilon = 1e-06


def merged(array, axis, combine):
    everything = jax.tree.map(
        lambda part, kind: lax.all_gather(part.astype(kind), axis),
        array,
        (jnp.bfloat16, jnp.bfloat16, jnp.bfloat16),
    )

    def take(k):
        return jax.tree.map(lambda part, own: part[k].astype(own.dtype), everything, array)

    return lax.fori_loop(
        1, lax.axis_size(axis), lambda k, so_far: combine(so_far, take(k)), take(0)
    )


def rms_norm(values, gain_vec):
    return values * lax.rsqrt(jnp.mean(values * values, -1, keepdims=True) + epsilon) * gain_vec


def pool_combine(first, second):
    max_one, sum_one, acc_one = first
    max_two, sum_two, acc_two = second
    top_value = jnp.maximum(max_one, max_two)
    left_factor = jnp.exp(max_one - top_value)
    right_factor = jnp.exp(max_two - top_value)
    return (
        top_value,
        sum_one * left_factor + sum_two * right_factor,
        acc_one * left_factor[:, None] + acc_two * right_factor[:, None],
    )


def body_gather(
    patches,
    var_embed,
    agg_query,
    pos_embed,
    gain_first,
    gain_second,
    w_qkv,
    w_out,
    w_dec,
    mod_scale,
    mod_shift,
):
    var_count = patches.shape[0]
    pos_rows = patches.shape[1]
    d_model = patches.shape[2]
    share_cols = d_model // lax.axis_size("chan")
    start_col = lax.axis_index("chan") * share_cols
    embedded = patches.astype(jnp.float32) + var_embed[:, None, :]
    logits = jnp.sum(embedded * agg_query, -1) * (1.0 / math.sqrt(D))
    local_top = jnp.max(logits, 0)
    expo_terms = jnp.exp(logits - local_top)
    part_sum = jnp.sum(expo_terms, 0)
    part_acc = jnp.sum(expo_terms[:, :, None] * embedded, 0)
    _, denom_sum, pooled_acc = merged((local_top, part_sum, part_acc), "chan", pool_combine)
    resid = pooled_acc / denom_sum[:, None] + pos_embed.astype(jnp.float32)
    normed = rms_norm(resid, gain_first).astype(jnp.bfloat16)
    columns = w_qkv.shape[2]
    qkv_all = jnp.dot(
        normed, w_qkv.reshape(d_model, 3 * columns), preferred_element_type=jnp.float32
    ).astype(jnp.bfloat16)
    head_dim = D // HEADS
    head_count = columns // head_dim
    queries = qkv_all[:, :columns].reshape(pos_rows, head_count, head_dim)
    keys_mine = qkv_all[:, columns : 2 * columns]
    values_mine = qkv_all[:, 2 * columns :]
    inv_scale = 1.0 / math.sqrt(head_dim)

    def attend_block(carry, key_block, value_block):
        run_max, run_sum, run_acc = carry
        scores = (
            jnp.einsum("phd,rhd->hpr", queries, key_block, preferred_element_type=jnp.float32)
            * inv_scale
        )
        new_max = jnp.maximum(run_max, jnp.max(scores, -1))
        rescale = jnp.exp(run_max - new_max)
        weights = jnp.exp(scores - new_max[..., None])
        run_sum = run_sum * rescale + jnp.sum(weights, -1)
        run_acc = run_acc * rescale[..., None] + jnp.einsum(
            "hpr,rhd->hpd",
            weights.astype(jnp.bfloat16),
            value_block,
            preferred_element_type=jnp.float32,
        )
        return (new_max, run_sum, run_acc)

    start_state = (
        jnp.full((head_count, pos_rows), -1e30, jnp.float32),
        jnp.zeros((head_count, pos_rows), jnp.float32),
        jnp.zeros((head_count, pos_rows, head_dim), jnp.float32),
    )
    key_piece = lax.all_gather(keys_mine, "space", axis=0, tiled=True)
    value_piece = lax.all_gather(values_mine, "space", axis=0, tiled=True)
    count_rows = key_piece.shape[0]
    key_heads = key_piece.reshape(count_rows, head_count, head_dim)
    value_heads = value_piece.reshape(count_rows, head_count, head_dim)
    blocks = count_rows // 1024
    key_stack = key_heads.reshape(blocks, 1024, head_count, head_dim)
    value_stack = value_heads.reshape(blocks, 1024, head_count, head_dim)

    def step_block(state, pair_in):
        return (attend_block(state, pair_in[0], pair_in[1]), None)

    result, _ = lax.scan(step_block, start_state, (key_stack, value_stack))
    run_max, run_sum, run_acc = result
    mixed = (
        (run_acc / run_sum[..., None])
        .transpose(1, 0, 2)
        .reshape(pos_rows, columns)
        .astype(jnp.bfloat16)
    )
    partial_out = jnp.dot(mixed, w_out, preferred_element_type=jnp.float32)
    share = lax.psum_scatter(
        partial_out.astype(jnp.bfloat16), "chan", scatter_dimension=1, tiled=True
    ).astype(jnp.float32)
    trunk_part = lax.dynamic_slice_in_dim(resid, start_col, share_cols, 1) + share
    square_sum = lax.psum(jnp.sum(trunk_part * trunk_part, 1), "chan")
    gain_part = lax.dynamic_slice_in_dim(gain_second, start_col, share_cols, 0)
    normed_part = (
        trunk_part * lax.rsqrt(square_sum[:, None] / d_model + epsilon) * gain_part
    ).astype(jnp.bfloat16)
    normed_two = lax.all_gather(normed_part, "chan", axis=1, tiled=True)
    modulated = (
        normed_two.astype(jnp.float32)[None] * (1.0 + mod_scale[:, None, :]) + mod_shift[:, None, :]
    ).astype(jnp.bfloat16)
    decoded = jnp.dot(
        modulated.reshape(var_count * pos_rows, d_model), w_dec, preferred_element_type=jnp.float32
    )
    return decoded.reshape(var_count, pos_rows, d_model).astype(jnp.bfloat16)


MESH = pl.DeviceIdType.MESH


def attention_kernel(
    chans, heads, qkv_ref, w_ref, mixed_ref, w_more_ref,
    got, part, k_rows, v_cols, score_a, score_b, stage,
    own_sem, send_sem, recv_sem, fwd_send, fwd_recv, out_send, out_recv,
    w_send, w_recv, w_fsend, w_frecv,
):
    space = lax.axis_index("space")
    chan = lax.axis_index("chan")
    chip = space // 2
    core = space % 2
    partner = chip * 2 + (1 - core)
    rows = qkv_ref.shape[3]
    head_dim = qkv_ref.shape[2]
    half = w_ref.shape[0] // 2

    def same_core(step):
        return lax.rem(chip + step, heads)

    barrier = pltpu.get_barrier_semaphore()
    count = 0
    for step in range(heads):
        for turn in range(chans):
            if step == 0 and turn == 0:
                continue
            pl.semaphore_signal(
                barrier, inc=1,
                device_id={"space": same_core(step) * 2 + core, "chan": lax.rem(chan + turn, chans)},
                device_id_type=MESH,
            )
            count += 1
    pl.semaphore_signal(barrier, inc=1, device_id={"space": partner}, device_id_type=MESH)
    pl.semaphore_wait(barrier, count + 1)

    def block_out(step):
        to = same_core(step)
        return pltpu.make_async_remote_copy(
            src_ref=qkv_ref.at[:, to], dst_ref=got.at[chip],
            send_sem=send_sem.at[step], recv_sem=recv_sem.at[chip],
            device_id={"space": to * 2 + core}, device_id_type=MESH,
        )

    def block_in(origin):
        return pltpu.make_async_remote_copy(
            src_ref=qkv_ref.at[:, chip], dst_ref=got.at[origin],
            send_sem=send_sem.at[0], recv_sem=recv_sem.at[origin],
            device_id={"space": partner}, device_id_type=MESH,
        )

    def forward(origin):
        return pltpu.make_async_remote_copy(
            src_ref=got.at[origin, pl.ds(1, 2)], dst_ref=part.at[origin],
            send_sem=fwd_send.at[origin], recv_sem=fwd_recv.at[origin],
            device_id={"space": partner}, device_id_type=MESH,
        )

    def w_out_copy(turn):
        return pltpu.make_async_remote_copy(
            src_ref=w_ref.at[pl.ds(core * half, half)],
            dst_ref=w_more_ref.at[chans - turn - 1, pl.ds(core * half, half)],
            send_sem=w_send.at[turn - 1], recv_sem=w_recv.at[chans - turn - 1],
            device_id={"chan": lax.rem(chan + turn, chans)}, device_id_type=MESH,
        )

    def w_forward(slot, which):
        return pltpu.make_async_remote_copy(
            src_ref=w_more_ref.at[slot, pl.ds(which * half, half)],
            dst_ref=w_more_ref.at[slot, pl.ds(which * half, half)],
            send_sem=w_fsend.at[slot], recv_sem=w_frecv.at[slot],
            device_id={"space": partner}, device_id_type=MESH,
        )

    own = pltpu.make_async_copy(qkv_ref.at[:, chip], got.at[chip], own_sem)
    own.start()
    for step in range(1, heads):
        block_out(step).start()
    for turn in range(1, chans):
        w_out_copy(turn).start()
    v_cols[:, pl.ds(head_dim, 16)] = jnp.ones_like(v_cols[:, pl.ds(head_dim, 16)])

    def take(slot, keys, values):
        k_rows[slot] = keys.T
        v_cols[slot, pl.ds(0, head_dim)] = values

    own.wait()
    forward(chip).start()
    take(chip, got[chip, 1], got[chip, 2])

    @pl.loop(1, heads)
    def _(step):
        origin = lax.rem(chip + heads - step, heads)
        block_in(origin).wait_recv()
        forward(origin).start()
        take(origin, got[origin, 1], got[origin, 2])

    for slot in range(chans - 1):
        w_out_copy(chans - 1 - slot).wait_recv()
        w_forward(slot, core).start()

    @pl.loop(0, heads)
    def _(step):
        origin = lax.rem(chip + heads - step, heads)
        forward(origin).wait_recv()
        take(heads + origin, part[origin, 0], part[origin, 1])

    blocks = 2 * heads

    def out_copy(step, turn):
        return pltpu.make_async_remote_copy(
            src_ref=stage.at[step], dst_ref=mixed_ref.at[(chans - turn) % chans, chip],
            send_sem=out_send.at[step, turn], recv_sem=out_recv.at[(chans - turn) % chans, chip],
            device_id={"space": same_core(step) * 2 + core, "chan": lax.rem(chan + turn, chans)},
            device_id_type=MESH,
        )

    def out_wait(shift, origin):
        return pltpu.make_async_remote_copy(
            src_ref=stage.at[0], dst_ref=mixed_ref.at[shift, origin],
            send_sem=out_send.at[0, 0], recv_sem=out_recv.at[shift, origin],
            device_id={"space": partner}, device_id_type=MESH,
        )

    def first_pass(step, scores):
        query = got[same_core(step), 0]

        def one(t, top):
            s = jnp.dot(k_rows[t], query, preferred_element_type=jnp.float32)
            scores[t] = s
            s_top = jnp.max(s.reshape(rows // 8, 8, rows), 0)
            return s_top if top is None else jnp.maximum(top, s_top)

        return one

    def second_pass(scores, top):
        def one(t, acc):
            p = jnp.exp2(scores[t] - top).astype(jnp.bfloat16)
            term = jnp.dot(v_cols[t], p, preferred_element_type=jnp.float32)
            return term if acc is None else acc + term

        return one

    def both(step, scores_now, top_now, scores_next):
        one_next = first_pass(step + 1, scores_next)
        one_now = second_pass(scores_now, top_now)
        top, acc = None, None
        for t in range(blocks):
            top = one_next(t, top)
            acc = one_now(t, acc)
        result = (acc[:head_dim] * (1.0 / acc[head_dim : head_dim + 1])).astype(jnp.bfloat16)
        stage[step] = result

        @pl.when(step == 0)
        def _():
            mixed_ref[0, chip] = result

        @pl.when(step != 0)
        def _():
            out_copy(step, 0).start()

        for turn in range(1, chans):
            out_copy(step, turn).start()
        return jnp.max(top, 0, keepdims=True)

    one = first_pass(0, score_a)
    top = None
    for t in range(blocks):
        top = one(t, top)
    top = jnp.max(top, 0, keepdims=True)

    def pair(i, top):
        top = both(2 * i, score_a, top, score_b)
        return both(2 * i + 1, score_b, top, score_a)

    lax.fori_loop(0, heads // 2, pair, top)

    for step in range(1, heads):
        block_out(step).wait_send()
        out_copy(step, 0).wait_send()
        out_wait(0, same_core(step)).wait_recv()
    for step in range(heads):
        forward(step).wait_send()
        for turn in range(1, chans):
            out_copy(step, turn).wait_send()
            out_wait(turn, step).wait_recv()
    for slot in range(chans - 1):
        w_out_copy(slot + 1).wait_send()
        w_forward(slot, core).wait_send()
        w_forward(slot, 1 - core).wait_recv()


def attention(qkv, w_out, chans):
    _, heads, head_dim, rows = qkv.shape
    dma = pltpu.SemaphoreType.DMA
    vmem = pl.BlockSpec(memory_space=pltpu.VMEM)
    hbm = pl.BlockSpec(memory_space=pl.ANY)
    bf16 = jnp.bfloat16
    return pl.pallas_call(
        functools.partial(attention_kernel, chans, heads),
        out_shape=(
            jax.ShapeDtypeStruct((chans, heads, head_dim, rows), bf16),
            jax.ShapeDtypeStruct((chans - 1,) + w_out.shape, bf16),
        ),
        in_specs=[vmem, hbm],
        out_specs=(vmem, hbm),
        scratch_shapes=[
            pltpu.VMEM((heads, 3, head_dim, rows), bf16),
            pltpu.VMEM((heads, 2, head_dim, rows), bf16),
            pltpu.VMEM((2 * heads, rows, head_dim), bf16),
            pltpu.VMEM((2 * heads, head_dim + 16, rows), bf16),
            pltpu.VMEM((2 * heads, rows, rows), jnp.float32),
            pltpu.VMEM((2 * heads, rows, rows), jnp.float32),
            pltpu.VMEM((heads, head_dim, rows), bf16),
            dma, dma((heads,)), dma((heads,)), dma((heads,)), dma((heads,)),
            dma((heads, chans)), dma((chans, heads)),
            dma((chans - 1,)), dma((chans - 1,)), dma((chans - 1,)), dma((chans - 1,)),
        ],
        compiler_params=pltpu.CompilerParams(
            collective_id=0, has_side_effects=True, vmem_limit_bytes=48 * 1024 * 1024
        ),
    )(qkv, w_out)


def body_exchange(
    patches,
    var_embed,
    agg_query,
    pos_embed,
    gain_first,
    gain_second,
    w_qkv,
    w_out,
    w_dec,
    mod_scale,
    mod_shift,
):
    var_count, pos_rows, d_model = patches.shape
    chans = lax.axis_size("chan")
    embedded = patches.astype(jnp.float32) + var_embed[:, None, :]
    logits = jnp.sum(embedded * agg_query, -1) * (1.0 / math.sqrt(D))
    local_top = jnp.max(logits, 0)
    expo_terms = jnp.exp(logits - local_top)
    part_sum = jnp.sum(expo_terms, 0)
    part_acc = jnp.sum(expo_terms[:, :, None] * embedded, 0)
    state = (local_top, part_sum, part_acc)
    sent = part_acc.astype(jnp.bfloat16)
    stats = jnp.stack([local_top, part_sum])
    for turn in range(1, chans):
        ring = [(i, (i + turn) % chans) for i in range(chans)]
        there = lax.ppermute(sent, "chan", ring).astype(jnp.float32)
        there_stats = lax.ppermute(stats, "chan", ring)
        state = pool_combine(state, (there_stats[0], there_stats[1], there))
    _, denom_sum, pooled_acc = state
    resid = pooled_acc / denom_sum[:, None] + pos_embed.astype(jnp.float32)
    normed = rms_norm(resid, gain_first).astype(jnp.bfloat16)
    columns = w_qkv.shape[2]
    head_dim = D // HEADS
    head_count = columns // head_dim
    factor = jnp.array([math.log2(math.e) / math.sqrt(head_dim), 1.0, 1.0], jnp.float32)
    qkv = lax.dot_general(
        w_qkv.reshape(d_model, 3 * columns), normed, (((0,), (1,)), ((), ())),
        preferred_element_type=jnp.float32,
    ).reshape(3, head_count, head_dim, pos_rows)
    qkv = (qkv * factor[:, None, None, None]).astype(jnp.bfloat16)
    mixed, w_more = attention(qkv, w_out, chans)
    mixed = mixed.reshape(chans, columns, pos_rows)
    trunk = resid
    for shift in range(chans):
        trunk = trunk + lax.dot_general(
            mixed[shift], w_out if shift == 0 else w_more[shift - 1], (((0,), (0,)), ((), ())),
            preferred_element_type=jnp.float32,
        )
    normed_two = rms_norm(trunk, gain_second).astype(jnp.bfloat16)
    modulated = (
        normed_two.astype(jnp.float32)[None] * (1.0 + mod_scale[:, None, :]) + mod_shift[:, None, :]
    ).astype(jnp.bfloat16)
    decoded = jnp.dot(
        modulated.reshape(var_count * pos_rows, d_model), w_dec, preferred_element_type=jnp.float32
    )
    return decoded.reshape(var_count, pos_rows, d_model).astype(jnp.bfloat16)


def solution(mesh):
    placed = (
        P("chan", "space", None),
        P("chan", None),
        P(),
        P("space", None),
        P(),
        P(),
        P(None, None, "chan"),
        P("chan", None),
        P(),
        P("chan", None),
        P("chan", None),
    )
    per_chan = HEADS // mesh.shape["chan"]
    body = body_exchange if mesh.shape["space"] == 2 * per_chan else body_gather
    return jax.shard_map(
        body, mesh=mesh, in_specs=placed, out_specs=P("chan", "space", None), check_vma=False
    )
```

```python
import functools
import math

import jax
import jax.numpy as jnp
from jax import lax
from jax.experimental import pallas as pl
from jax.experimental.pallas import tpu as pltpu
from jax.sharding import PartitionSpec as P

D = 1024
HEADS = 16


epsilon = 1e-06


def merged(array, axis, combine):
    everything = jax.tree.map(
        lambda part, kind: lax.all_gather(part.astype(kind), axis),
        array,
        (jnp.bfloat16, jnp.bfloat16, jnp.bfloat16),
    )

    def take(k):
        return jax.tree.map(lambda part, own: part[k].astype(own.dtype), everything, array)

    return lax.fori_loop(
        1, lax.axis_size(axis), lambda k, so_far: combine(so_far, take(k)), take(0)
    )


def rms_norm(values, gain_vec):
    return values * lax.rsqrt(jnp.mean(values * values, -1, keepdims=True) + epsilon) * gain_vec


def pool_combine(first, second):
    max_one, sum_one, acc_one = first
    max_two, sum_two, acc_two = second
    top_value = jnp.maximum(max_one, max_two)
    left_factor = jnp.exp(max_one - top_value)
    right_factor = jnp.exp(max_two - top_value)
    return (
        top_value,
        sum_one * left_factor + sum_two * right_factor,
        acc_one * left_factor[:, None] + acc_two * right_factor[:, None],
    )


def body_gather(
    patches,
    var_embed,
    agg_query,
    pos_embed,
    gain_first,
    gain_second,
    w_qkv,
    w_out,
    w_dec,
    mod_scale,
    mod_shift,
):
    var_count = patches.shape[0]
    pos_rows = patches.shape[1]
    d_model = patches.shape[2]
    share_cols = d_model // lax.axis_size("chan")
    start_col = lax.axis_index("chan") * share_cols
    embedded = patches.astype(jnp.float32) + var_embed[:, None, :]
    logits = jnp.sum(embedded * agg_query, -1) * (1.0 / math.sqrt(D))
    local_top = jnp.max(logits, 0)
    expo_terms = jnp.exp(logits - local_top)
    part_sum = jnp.sum(expo_terms, 0)
    part_acc = jnp.sum(expo_terms[:, :, None] * embedded, 0)
    _, denom_sum, pooled_acc = merged((local_top, part_sum, part_acc), "chan", pool_combine)
    resid = pooled_acc / denom_sum[:, None] + pos_embed.astype(jnp.float32)
    normed = rms_norm(resid, gain_first).astype(jnp.bfloat16)
    columns = w_qkv.shape[2]
    qkv_all = jnp.dot(
        normed, w_qkv.reshape(d_model, 3 * columns), preferred_element_type=jnp.float32
    ).astype(jnp.bfloat16)
    head_dim = D // HEADS
    head_count = columns // head_dim
    queries = qkv_all[:, :columns].reshape(pos_rows, head_count, head_dim)
    keys_mine = qkv_all[:, columns : 2 * columns]
    values_mine = qkv_all[:, 2 * columns :]
    inv_scale = 1.0 / math.sqrt(head_dim)

    def attend_block(carry, key_block, value_block):
        run_max, run_sum, run_acc = carry
        scores = (
            jnp.einsum("phd,rhd->hpr", queries, key_block, preferred_element_type=jnp.float32)
            * inv_scale
        )
        new_max = jnp.maximum(run_max, jnp.max(scores, -1))
        rescale = jnp.exp(run_max - new_max)
        weights = jnp.exp(scores - new_max[..., None])
        run_sum = run_sum * rescale + jnp.sum(weights, -1)
        run_acc = run_acc * rescale[..., None] + jnp.einsum(
            "hpr,rhd->hpd",
            weights.astype(jnp.bfloat16),
            value_block,
            preferred_element_type=jnp.float32,
        )
        return (new_max, run_sum, run_acc)

    start_state = (
        jnp.full((head_count, pos_rows), -1e30, jnp.float32),
        jnp.zeros((head_count, pos_rows), jnp.float32),
        jnp.zeros((head_count, pos_rows, head_dim), jnp.float32),
    )
    key_piece = lax.all_gather(keys_mine, "space", axis=0, tiled=True)
    value_piece = lax.all_gather(values_mine, "space", axis=0, tiled=True)
    count_rows = key_piece.shape[0]
    key_heads = key_piece.reshape(count_rows, head_count, head_dim)
    value_heads = value_piece.reshape(count_rows, head_count, head_dim)
    blocks = count_rows // 1024
    key_stack = key_heads.reshape(blocks, 1024, head_count, head_dim)
    value_stack = value_heads.reshape(blocks, 1024, head_count, head_dim)

    def step_block(state, pair_in):
        return (attend_block(state, pair_in[0], pair_in[1]), None)

    result, _ = lax.scan(step_block, start_state, (key_stack, value_stack))
    run_max, run_sum, run_acc = result
    mixed = (
        (run_acc / run_sum[..., None])
        .transpose(1, 0, 2)
        .reshape(pos_rows, columns)
        .astype(jnp.bfloat16)
    )
    partial_out = jnp.dot(mixed, w_out, preferred_element_type=jnp.float32)
    share = lax.psum_scatter(
        partial_out.astype(jnp.bfloat16), "chan", scatter_dimension=1, tiled=True
    ).astype(jnp.float32)
    trunk_part = lax.dynamic_slice_in_dim(resid, start_col, share_cols, 1) + share
    square_sum = lax.psum(jnp.sum(trunk_part * trunk_part, 1), "chan")
    gain_part = lax.dynamic_slice_in_dim(gain_second, start_col, share_cols, 0)
    normed_part = (
        trunk_part * lax.rsqrt(square_sum[:, None] / d_model + epsilon) * gain_part
    ).astype(jnp.bfloat16)
    normed_two = lax.all_gather(normed_part, "chan", axis=1, tiled=True)
    modulated = (
        normed_two.astype(jnp.float32)[None] * (1.0 + mod_scale[:, None, :]) + mod_shift[:, None, :]
    ).astype(jnp.bfloat16)
    decoded = jnp.dot(
        modulated.reshape(var_count * pos_rows, d_model), w_dec, preferred_element_type=jnp.float32
    )
    return decoded.reshape(var_count, pos_rows, d_model).astype(jnp.bfloat16)


MESH = pl.DeviceIdType.MESH
PARTS = 4


def fused_kernel(
    chans, heads,
    patches_ref, embed_ref, query_ref, pos_ref, gain_ref, w_qkv_ref, w_ref,
    mixed_ref, w_more_ref, resid_ref,
    tokens, w_qkv, pos, acc, acc_out, acc_in, stat, stat_in, acc_stat, normed, qkv_ref,
    got, part, k_rows, v_cols, score_a, score_b, stage,
    load_sem, acc_send, acc_recv, stat_send, stat_recv,
    send_sem, recv_sem, fwd_send, fwd_recv, out_send, out_recv,
    w_send, w_recv, w_fsend, w_frecv,
):
    space = lax.axis_index("space")
    chan = lax.axis_index("chan")
    chip = space // 2
    core = space % 2
    partner = chip * 2 + (1 - core)
    var_count, rows, d_model = tokens.shape
    head_dim = qkv_ref.shape[2]
    columns = heads * head_dim
    half = w_ref.shape[0] // 2
    part_rows = rows // PARTS
    half_rows = rows // 2

    def same_core(step):
        return lax.rem(chip + step, heads)

    loads = [
        pltpu.make_async_copy(
            patches_ref.at[:, pl.ds(c * part_rows, part_rows)],
            tokens.at[:, pl.ds(c * part_rows, part_rows)], load_sem.at[c],
        )
        for c in range(PARTS)
    ]
    load_w = pltpu.make_async_copy(w_qkv_ref, w_qkv, load_sem.at[PARTS])
    load_pos = pltpu.make_async_copy(pos_ref, pos, load_sem.at[PARTS + 1])
    for copy in loads + [load_pos, load_w]:
        copy.start()

    barrier = pltpu.get_barrier_semaphore()
    count = 0
    for step in range(heads):
        for turn in range(chans):
            if step == 0 and turn == 0:
                continue
            pl.semaphore_signal(
                barrier, inc=1,
                device_id={"space": same_core(step) * 2 + core, "chan": lax.rem(chan + turn, chans)},
                device_id_type=MESH,
            )
            count += 1
    pl.semaphore_signal(barrier, inc=1, device_id={"space": partner}, device_id_type=MESH)

    def acc_copy(c, turn):
        place = pl.ds(c * part_rows, part_rows)
        return pltpu.make_async_remote_copy(
            src_ref=acc_out.at[place], dst_ref=acc_in.at[chans - turn - 1, place],
            send_sem=acc_send.at[c, turn - 1], recv_sem=acc_recv.at[c, chans - turn - 1],
            device_id={"chan": lax.rem(chan + turn, chans)}, device_id_type=MESH,
        )

    def stat_copy(h, turn):
        return pltpu.make_async_remote_copy(
            src_ref=stat.at[h, pl.ds(0, 8)], dst_ref=stat_in.at[h, chans - turn - 1],
            send_sem=stat_send.at[h, turn - 1], recv_sem=stat_recv.at[h, chans - turn - 1],
            device_id={"chan": lax.rem(chan + turn, chans)}, device_id_type=MESH,
        )

    def lanes_of(h):
        return pl.ds(h * half_rows, half_rows)

    def block_out(h, step):
        to = same_core(step)
        return pltpu.make_async_remote_copy(
            src_ref=qkv_ref.at[:, to, :, lanes_of(h)], dst_ref=got.at[chip, :, :, lanes_of(h)],
            send_sem=send_sem.at[h, step], recv_sem=recv_sem.at[h, chip],
            device_id={"space": to * 2 + core}, device_id_type=MESH,
        )

    def block_in(h, origin):
        return pltpu.make_async_remote_copy(
            src_ref=qkv_ref.at[:, chip, :, lanes_of(h)], dst_ref=got.at[origin, :, :, lanes_of(h)],
            send_sem=send_sem.at[h, 0], recv_sem=recv_sem.at[h, origin],
            device_id={"space": partner}, device_id_type=MESH,
        )

    def forward(h, origin):
        return pltpu.make_async_remote_copy(
            src_ref=got.at[origin, pl.ds(1, 2), :, lanes_of(h)],
            dst_ref=part.at[origin, :, :, lanes_of(h)],
            send_sem=fwd_send.at[h, origin], recv_sem=fwd_recv.at[h, origin],
            device_id={"space": partner}, device_id_type=MESH,
        )

    def w_out_copy(turn):
        return pltpu.make_async_remote_copy(
            src_ref=w_ref.at[pl.ds(core * half, half)],
            dst_ref=w_more_ref.at[chans - turn - 1, pl.ds(core * half, half)],
            send_sem=w_send.at[turn - 1], recv_sem=w_recv.at[chans - turn - 1],
            device_id={"chan": lax.rem(chan + turn, chans)}, device_id_type=MESH,
        )

    def w_forward(slot, which):
        return pltpu.make_async_remote_copy(
            src_ref=w_more_ref.at[slot, pl.ds(which * half, half)],
            dst_ref=w_more_ref.at[slot, pl.ds(which * half, half)],
            send_sem=w_fsend.at[slot], recv_sem=w_frecv.at[slot],
            device_id={"space": partner}, device_id_type=MESH,
        )

    v_cols[:, pl.ds(head_dim, 16)] = jnp.ones_like(v_cols[:, pl.ds(head_dim, 16)])
    group = 16
    lane = lax.broadcasted_iota(jnp.int32, (group, 128), 1)
    agg_query = query_ref[...]

    def pool(c):
        @pl.loop(0, part_rows // group)
        def _(i):
            at = pl.ds(pl.multiple_of(c * part_rows + i * group, group), group)
            logits = []
            for v in range(var_count):
                embedded = tokens[v, at].astype(jnp.float32) + embed_ref[pl.ds(v, 1)]
                logits.append(
                    jnp.sum(embedded * agg_query, -1, keepdims=True) * (1.0 / math.sqrt(D))
                )
            top = functools.reduce(jnp.maximum, logits)
            total, weighted = None, None
            for v in range(var_count):
                embedded = tokens[v, at].astype(jnp.float32) + embed_ref[pl.ds(v, 1)]
                weight = jnp.exp(logits[v] - top)
                total = weight if v == 0 else total + weight
                weighted = weight * embedded if v == 0 else weighted + weight * embedded
            acc[at] = weighted
            acc_out[at] = weighted.astype(jnp.bfloat16)
            resid_ref[at, pl.ds(0, 128)] = jnp.where(lane == 0, top, total)

    for c in range(PARTS):
        loads[c].wait()
        pool(c)
        if c == 0:
            pl.semaphore_wait(barrier, count + 1)
        for turn in range(1, chans):
            acc_copy(c, turn).start()
        if c % (PARTS // 2) == PARTS // 2 - 1:
            h = c // (PARTS // 2)
            stat[h] = resid_ref[lanes_of(h), pl.ds(0, 128)].T
            for turn in range(1, chans):
                stat_copy(h, turn).start()

    def take(slot, h, keys, values):
        k_rows[slot, lanes_of(h)] = keys.T
        v_cols[slot, pl.ds(0, head_dim), lanes_of(h)] = values

    load_pos.wait()
    gain = gain_ref[...]
    spread = 128
    for h in range(2):
        for slot in range(chans - 1):
            stat_copy(h, chans - 1 - slot).wait_recv()
            for c in range(h * PARTS // 2, (h + 1) * PARTS // 2):
                acc_copy(c, chans - 1 - slot).wait_recv()

        for slot in range(chans - 1):
            stat_ref = stat_in.at[h, slot]
            wide = jnp.concatenate([stat_ref[...]] * (spread // 8), 0).T
            acc_stat[slot] = wide

        @pl.loop(0, half_rows // group)
        def _(i):
            near = pl.ds(pl.multiple_of(i * group, group), group)
            at = pl.ds(pl.multiple_of(h * half_rows + i * group, group), group)
            own = resid_ref[at, pl.ds(0, 128)]
            tops, totals = [own[:, 0:1]], [own[:, 1:2]]
            for slot in range(chans - 1):
                other = acc_stat[slot, near]
                tops.append(other[:, 0:1])
                totals.append(other[:, 1:2])
            top = functools.reduce(jnp.maximum, tops)
            factors = [jnp.exp(t - top) for t in tops]
            denom = functools.reduce(jnp.add, [f * t for f, t in zip(factors, totals)])
            pooled = acc[at] * (factors[0] / denom)
            for slot in range(chans - 1):
                pooled += acc_in[slot, at].astype(jnp.float32) * (factors[slot + 1] / denom)
            resid = pooled + pos[at].astype(jnp.float32)
            resid_ref[at] = resid
            normed[near] = rms_norm(resid, gain).astype(jnp.bfloat16)

        if h == 0:
            load_w.wait()
        for j in range(3):
            out = jnp.dot(
                normed[...], w_qkv[:, pl.ds(j * columns, columns)],
                preferred_element_type=jnp.float32,
            )
            if j == 0:
                out = out * (math.log2(math.e) / math.sqrt(head_dim))
            qkv_ref[j, :, :, lanes_of(h)] = (
                out.T.astype(jnp.bfloat16).reshape(heads, head_dim, half_rows)
            )
        for step in range(1, heads):
            block_out(h, step).start()
        got[chip, :, :, lanes_of(h)] = qkv_ref[:, chip, :, lanes_of(h)]
        forward(h, chip).start()
        take(chip, h, got[chip, 1, :, lanes_of(h)], got[chip, 2, :, lanes_of(h)])

    for turn in range(1, chans):
        w_out_copy(turn).start()

    for h in range(2):
        @pl.loop(1, heads)
        def _(step):
            origin = lax.rem(chip + heads - step, heads)
            block_in(h, origin).wait_recv()
            forward(h, origin).start()
            take(origin, h, got[origin, 1, :, lanes_of(h)], got[origin, 2, :, lanes_of(h)])

    for h in range(2):
        @pl.loop(0, heads)
        def _(step):
            origin = lax.rem(chip + heads - step, heads)
            forward(h, origin).wait_recv()
            take(
                heads + origin, h, part[origin, 0, :, lanes_of(h)], part[origin, 1, :, lanes_of(h)]
            )

    blocks = 2 * heads

    def out_copy(step, turn):
        return pltpu.make_async_remote_copy(
            src_ref=stage.at[step], dst_ref=mixed_ref.at[(chans - turn) % chans, chip],
            send_sem=out_send.at[step, turn], recv_sem=out_recv.at[(chans - turn) % chans, chip],
            device_id={"space": same_core(step) * 2 + core, "chan": lax.rem(chan + turn, chans)},
            device_id_type=MESH,
        )

    def out_wait(shift, origin):
        return pltpu.make_async_remote_copy(
            src_ref=stage.at[0], dst_ref=mixed_ref.at[shift, origin],
            send_sem=out_send.at[0, 0], recv_sem=out_recv.at[shift, origin],
            device_id={"space": partner}, device_id_type=MESH,
        )

    def first_pass(step, scores):
        query = got[same_core(step), 0]

        def one(t, top):
            s = jnp.dot(k_rows[t], query, preferred_element_type=jnp.float32)
            scores[t] = s
            s_top = jnp.max(s.reshape(rows // 8, 8, rows), 0)
            return s_top if top is None else jnp.maximum(top, s_top)

        return one

    def second_pass(scores, top):
        def one(t, acc):
            p = jnp.exp2(scores[t] - top).astype(jnp.bfloat16)
            term = jnp.dot(v_cols[t], p, preferred_element_type=jnp.float32)
            return term if acc is None else acc + term

        return one

    def both(step, scores_now, top_now, scores_next):
        one_next = first_pass(step + 1, scores_next)
        one_now = second_pass(scores_now, top_now)
        top, acc = None, None
        for t in range(blocks):
            top = one_next(t, top)
            acc = one_now(t, acc)
        result = (acc[:head_dim] * (1.0 / acc[head_dim : head_dim + 1])).astype(jnp.bfloat16)
        stage[step] = result

        @pl.when(step == 0)
        def _():
            mixed_ref[0, chip] = result

        @pl.when(step != 0)
        def _():
            out_copy(step, 0).start()

        for turn in range(1, chans):
            out_copy(step, turn).start()
        return jnp.max(top, 0, keepdims=True)

    one = first_pass(0, score_a)
    top = None
    for t in range(blocks):
        top = one(t, top)
    top = jnp.max(top, 0, keepdims=True)

    def pair(i, top):
        top = both(2 * i, score_a, top, score_b)
        return both(2 * i + 1, score_b, top, score_a)

    top = lax.fori_loop(0, heads // 4, pair, top)
    for slot in range(chans - 1):
        w_out_copy(chans - 1 - slot).wait_recv()
        w_forward(slot, core).start()
    lax.fori_loop(heads // 4, heads // 2, pair, top)

    for step in range(1, heads):
        for h in range(2):
            block_out(h, step).wait_send()
        out_copy(step, 0).wait_send()
        out_wait(0, same_core(step)).wait_recv()
    for step in range(heads):
        for h in range(2):
            forward(h, step).wait_send()
        for turn in range(1, chans):
            out_copy(step, turn).wait_send()
            out_wait(turn, step).wait_recv()
    for slot in range(chans - 1):
        w_out_copy(slot + 1).wait_send()
        w_forward(slot, core).wait_send()
        w_forward(slot, 1 - core).wait_recv()
        for c in range(PARTS):
            acc_copy(c, slot + 1).wait_send()
        for h in range(2):
            stat_copy(h, slot + 1).wait_send()


def fused(patches, var_embed, agg_query, pos_embed, gain_first, w_qkv, w_out, chans):
    var_count, rows, d_model = patches.shape
    columns = w_qkv.shape[1] // 3
    head_dim = D // HEADS
    heads = columns // head_dim
    dma = pltpu.SemaphoreType.DMA
    vmem = pl.BlockSpec(memory_space=pltpu.VMEM)
    hbm = pl.BlockSpec(memory_space=pl.ANY)
    bf16, f32 = jnp.bfloat16, jnp.float32
    return pl.pallas_call(
        functools.partial(fused_kernel, chans, heads),
        out_shape=(
            jax.ShapeDtypeStruct((chans, heads, head_dim, rows), bf16),
            jax.ShapeDtypeStruct((chans - 1,) + w_out.shape, bf16),
            jax.ShapeDtypeStruct((rows, d_model), f32),
        ),
        in_specs=[hbm, vmem, vmem, hbm, vmem, hbm, hbm],
        out_specs=(vmem, hbm, vmem),
        scratch_shapes=[
            pltpu.VMEM(patches.shape, bf16),
            pltpu.VMEM(w_qkv.shape, bf16),
            pltpu.VMEM((rows, d_model), bf16),
            pltpu.VMEM((rows, d_model), f32),
            pltpu.VMEM((rows, d_model), bf16),
            pltpu.VMEM((chans - 1, rows, d_model), bf16),
            pltpu.VMEM((2, 128, rows // 2), f32),
            pltpu.VMEM((2, chans - 1, 8, rows // 2), f32),
            pltpu.VMEM((chans - 1, rows // 2, 128), f32),
            pltpu.VMEM((rows // 2, d_model), bf16),
            pltpu.VMEM((3, heads, head_dim, rows), bf16),
            pltpu.VMEM((heads, 3, head_dim, rows), bf16),
            pltpu.VMEM((heads, 2, head_dim, rows), bf16),
            pltpu.VMEM((2 * heads, rows, head_dim), bf16),
            pltpu.VMEM((2 * heads, head_dim + 16, rows), bf16),
            pltpu.VMEM((2 * heads, rows, rows), f32),
            pltpu.VMEM((2 * heads, rows, rows), f32),
            pltpu.VMEM((heads, head_dim, rows), bf16),
            dma((PARTS + 2,)),
            dma((PARTS, chans - 1)), dma((PARTS, chans - 1)),
            dma((2, chans - 1)), dma((2, chans - 1)),
            dma((2, heads)), dma((2, heads)), dma((2, heads)), dma((2, heads)),
            dma((heads, chans)), dma((chans, heads)),
            dma((chans - 1,)), dma((chans - 1,)), dma((chans - 1,)), dma((chans - 1,)),
        ],
        compiler_params=pltpu.CompilerParams(
            collective_id=0, has_side_effects=True, vmem_limit_bytes=56 * 1024 * 1024
        ),
    )(patches, var_embed, agg_query[None], pos_embed, gain_first[None], w_qkv, w_out)


def body_exchange(
    patches,
    var_embed,
    agg_query,
    pos_embed,
    gain_first,
    gain_second,
    w_qkv,
    w_out,
    w_dec,
    mod_scale,
    mod_shift,
):
    var_count, pos_rows, d_model = patches.shape
    chans = lax.axis_size("chan")
    columns = w_qkv.shape[2]
    mixed, w_more, resid = fused(
        patches, var_embed, agg_query, pos_embed, gain_first,
        w_qkv.reshape(d_model, 3 * columns), w_out, chans,
    )
    mixed = mixed.reshape(chans, columns, pos_rows)
    trunk = resid
    for shift in range(chans):
        trunk = trunk + lax.dot_general(
            mixed[shift], w_out if shift == 0 else w_more[shift - 1], (((0,), (0,)), ((), ())),
            preferred_element_type=jnp.float32,
        )
    normed_two = rms_norm(trunk, gain_second).astype(jnp.bfloat16)
    modulated = (
        normed_two.astype(jnp.float32)[None] * (1.0 + mod_scale[:, None, :]) + mod_shift[:, None, :]
    ).astype(jnp.bfloat16)
    decoded = jnp.dot(
        modulated.reshape(var_count * pos_rows, d_model), w_dec, preferred_element_type=jnp.float32
    )
    return decoded.reshape(var_count, pos_rows, d_model).astype(jnp.bfloat16)


def solution(mesh):
    placed = (
        P("chan", "space", None),
        P("chan", None),
        P(),
        P("space", None),
        P(),
        P(),
        P(None, None, "chan"),
        P("chan", None),
        P(),
        P("chan", None),
        P("chan", None),
    )
    per_chan = HEADS // mesh.shape["chan"]
    body = body_exchange if mesh.shape["space"] == 2 * per_chan else body_gather
    return jax.shard_map(
        body, mesh=mesh, in_specs=placed, out_specs=P("chan", "space", None), check_vma=False
    )
```

```python
import functools
import math

import jax
import jax.numpy as jnp
from jax import lax
from jax.experimental import pallas as pl
from jax.experimental.pallas import tpu as pltpu
from jax.sharding import PartitionSpec as P

D = 1024
HEADS = 16


epsilon = 1e-06


def merged(array, axis, combine):
    everything = jax.tree.map(
        lambda part, kind: lax.all_gather(part.astype(kind), axis),
        array,
        (jnp.bfloat16, jnp.bfloat16, jnp.bfloat16),
    )

    def take(k):
        return jax.tree.map(lambda part, own: part[k].astype(own.dtype), everything, array)

    return lax.fori_loop(
        1, lax.axis_size(axis), lambda k, so_far: combine(so_far, take(k)), take(0)
    )


def rms_norm(values, gain_vec):
    return values * lax.rsqrt(jnp.mean(values * values, -1, keepdims=True) + epsilon) * gain_vec


def pool_combine(first, second):
    max_one, sum_one, acc_one = first
    max_two, sum_two, acc_two = second
    top_value = jnp.maximum(max_one, max_two)
    left_factor = jnp.exp(max_one - top_value)
    right_factor = jnp.exp(max_two - top_value)
    return (
        top_value,
        sum_one * left_factor + sum_two * right_factor,
        acc_one * left_factor[:, None] + acc_two * right_factor[:, None],
    )


def body_gather(
    patches,
    var_embed,
    agg_query,
    pos_embed,
    gain_first,
    gain_second,
    w_qkv,
    w_out,
    w_dec,
    mod_scale,
    mod_shift,
):
    var_count = patches.shape[0]
    pos_rows = patches.shape[1]
    d_model = patches.shape[2]
    share_cols = d_model // lax.axis_size("chan")
    start_col = lax.axis_index("chan") * share_cols
    embedded = patches.astype(jnp.float32) + var_embed[:, None, :]
    logits = jnp.sum(embedded * agg_query, -1) * (1.0 / math.sqrt(D))
    local_top = jnp.max(logits, 0)
    expo_terms = jnp.exp(logits - local_top)
    part_sum = jnp.sum(expo_terms, 0)
    part_acc = jnp.sum(expo_terms[:, :, None] * embedded, 0)
    _, denom_sum, pooled_acc = merged((local_top, part_sum, part_acc), "chan", pool_combine)
    resid = pooled_acc / denom_sum[:, None] + pos_embed.astype(jnp.float32)
    normed = rms_norm(resid, gain_first).astype(jnp.bfloat16)
    columns = w_qkv.shape[2]
    qkv_all = jnp.dot(
        normed, w_qkv.reshape(d_model, 3 * columns), preferred_element_type=jnp.float32
    ).astype(jnp.bfloat16)
    head_dim = D // HEADS
    head_count = columns // head_dim
    queries = qkv_all[:, :columns].reshape(pos_rows, head_count, head_dim)
    keys_mine = qkv_all[:, columns : 2 * columns]
    values_mine = qkv_all[:, 2 * columns :]
    inv_scale = 1.0 / math.sqrt(head_dim)

    def attend_block(carry, key_block, value_block):
        run_max, run_sum, run_acc = carry
        scores = (
            jnp.einsum("phd,rhd->hpr", queries, key_block, preferred_element_type=jnp.float32)
            * inv_scale
        )
        new_max = jnp.maximum(run_max, jnp.max(scores, -1))
        rescale = jnp.exp(run_max - new_max)
        weights = jnp.exp(scores - new_max[..., None])
        run_sum = run_sum * rescale + jnp.sum(weights, -1)
        run_acc = run_acc * rescale[..., None] + jnp.einsum(
            "hpr,rhd->hpd",
            weights.astype(jnp.bfloat16),
            value_block,
            preferred_element_type=jnp.float32,
        )
        return (new_max, run_sum, run_acc)

    start_state = (
        jnp.full((head_count, pos_rows), -1e30, jnp.float32),
        jnp.zeros((head_count, pos_rows), jnp.float32),
        jnp.zeros((head_count, pos_rows, head_dim), jnp.float32),
    )
    key_piece = lax.all_gather(keys_mine, "space", axis=0, tiled=True)
    value_piece = lax.all_gather(values_mine, "space", axis=0, tiled=True)
    count_rows = key_piece.shape[0]
    key_heads = key_piece.reshape(count_rows, head_count, head_dim)
    value_heads = value_piece.reshape(count_rows, head_count, head_dim)
    blocks = count_rows // 1024
    key_stack = key_heads.reshape(blocks, 1024, head_count, head_dim)
    value_stack = value_heads.reshape(blocks, 1024, head_count, head_dim)

    def step_block(state, pair_in):
        return (attend_block(state, pair_in[0], pair_in[1]), None)

    result, _ = lax.scan(step_block, start_state, (key_stack, value_stack))
    run_max, run_sum, run_acc = result
    mixed = (
        (run_acc / run_sum[..., None])
        .transpose(1, 0, 2)
        .reshape(pos_rows, columns)
        .astype(jnp.bfloat16)
    )
    partial_out = jnp.dot(mixed, w_out, preferred_element_type=jnp.float32)
    share = lax.psum_scatter(
        partial_out.astype(jnp.bfloat16), "chan", scatter_dimension=1, tiled=True
    ).astype(jnp.float32)
    trunk_part = lax.dynamic_slice_in_dim(resid, start_col, share_cols, 1) + share
    square_sum = lax.psum(jnp.sum(trunk_part * trunk_part, 1), "chan")
    gain_part = lax.dynamic_slice_in_dim(gain_second, start_col, share_cols, 0)
    normed_part = (
        trunk_part * lax.rsqrt(square_sum[:, None] / d_model + epsilon) * gain_part
    ).astype(jnp.bfloat16)
    normed_two = lax.all_gather(normed_part, "chan", axis=1, tiled=True)
    modulated = (
        normed_two.astype(jnp.float32)[None] * (1.0 + mod_scale[:, None, :]) + mod_shift[:, None, :]
    ).astype(jnp.bfloat16)
    decoded = jnp.dot(
        modulated.reshape(var_count * pos_rows, d_model), w_dec, preferred_element_type=jnp.float32
    )
    return decoded.reshape(var_count, pos_rows, d_model).astype(jnp.bfloat16)


MESH = pl.DeviceIdType.MESH
PARTS = 4


def fused_kernel(
    chans, heads,
    patches_ref, embed_ref, query_ref, pos_ref, gain_ref, w_qkv_ref, w_ref,
    mixed_ref, w_more_ref, resid_ref,
    tokens, w_qkv, pos, acc, acc_out, acc_in, stat, stat_in, acc_stat, normed, qkv_ref,
    got, part, k_rows, v_cols, score_a, score_b, stage,
    load_sem, acc_send, acc_recv, stat_send, stat_recv,
    send_sem, recv_sem, fwd_send, fwd_recv, out_send, out_recv,
    w_send, w_recv, w_fsend, w_frecv,
):
    space = lax.axis_index("space")
    chan = lax.axis_index("chan")
    chip = space // 2
    core = space % 2
    partner = chip * 2 + (1 - core)
    var_count, rows, d_model = tokens.shape
    head_dim = qkv_ref.shape[2]
    columns = heads * head_dim
    half = w_ref.shape[0] // 2
    part_rows = rows // PARTS
    half_rows = rows // 2

    def same_core(step):
        return lax.rem(chip + step, heads)

    loads = [
        pltpu.make_async_copy(
            patches_ref.at[:, pl.ds(c * part_rows, part_rows)],
            tokens.at[:, pl.ds(c * part_rows, part_rows)], load_sem.at[c],
        )
        for c in range(PARTS)
    ]
    load_w = pltpu.make_async_copy(w_qkv_ref, w_qkv, load_sem.at[PARTS])
    load_pos = pltpu.make_async_copy(pos_ref, pos, load_sem.at[PARTS + 1])
    for copy in loads + [load_pos, load_w]:
        copy.start()

    barrier = pltpu.get_barrier_semaphore()
    count = 0
    for step in range(heads):
        for turn in range(chans):
            if step == 0 and turn == 0:
                continue
            pl.semaphore_signal(
                barrier, inc=1,
                device_id={"space": same_core(step) * 2 + core, "chan": lax.rem(chan + turn, chans)},
                device_id_type=MESH,
            )
            count += 1
    pl.semaphore_signal(barrier, inc=1, device_id={"space": partner}, device_id_type=MESH)

    def acc_copy(c, turn):
        place = pl.ds(c * part_rows, part_rows)
        return pltpu.make_async_remote_copy(
            src_ref=acc_out.at[place], dst_ref=acc_in.at[chans - turn - 1, place],
            send_sem=acc_send.at[c, turn - 1], recv_sem=acc_recv.at[c, chans - turn - 1],
            device_id={"chan": lax.rem(chan + turn, chans)}, device_id_type=MESH,
        )

    def stat_copy(h, turn):
        return pltpu.make_async_remote_copy(
            src_ref=stat.at[h, pl.ds(0, 8)], dst_ref=stat_in.at[h, chans - turn - 1],
            send_sem=stat_send.at[h, turn - 1], recv_sem=stat_recv.at[h, chans - turn - 1],
            device_id={"chan": lax.rem(chan + turn, chans)}, device_id_type=MESH,
        )

    def lanes_of(h):
        return pl.ds(h * half_rows, half_rows)

    def block_out(h, step):
        to = same_core(step)
        return pltpu.make_async_remote_copy(
            src_ref=qkv_ref.at[:, to, :, lanes_of(h)], dst_ref=got.at[chip, :, :, lanes_of(h)],
            send_sem=send_sem.at[h, step], recv_sem=recv_sem.at[h, chip],
            device_id={"space": to * 2 + core}, device_id_type=MESH,
        )

    def block_in(h, origin):
        return pltpu.make_async_remote_copy(
            src_ref=qkv_ref.at[:, chip, :, lanes_of(h)], dst_ref=got.at[origin, :, :, lanes_of(h)],
            send_sem=send_sem.at[h, 0], recv_sem=recv_sem.at[h, origin],
            device_id={"space": partner}, device_id_type=MESH,
        )

    def forward(h, origin):
        return pltpu.make_async_remote_copy(
            src_ref=got.at[origin, pl.ds(1, 2), :, lanes_of(h)],
            dst_ref=part.at[origin, :, :, lanes_of(h)],
            send_sem=fwd_send.at[h, origin], recv_sem=fwd_recv.at[h, origin],
            device_id={"space": partner}, device_id_type=MESH,
        )

    def w_out_copy(turn):
        return pltpu.make_async_remote_copy(
            src_ref=w_ref.at[pl.ds(core * half, half)],
            dst_ref=w_more_ref.at[chans - turn - 1, pl.ds(core * half, half)],
            send_sem=w_send.at[turn - 1], recv_sem=w_recv.at[chans - turn - 1],
            device_id={"chan": lax.rem(chan + turn, chans)}, device_id_type=MESH,
        )

    def w_forward(slot, which):
        return pltpu.make_async_remote_copy(
            src_ref=w_more_ref.at[slot, pl.ds(which * half, half)],
            dst_ref=w_more_ref.at[slot, pl.ds(which * half, half)],
            send_sem=w_fsend.at[slot], recv_sem=w_frecv.at[slot],
            device_id={"space": partner}, device_id_type=MESH,
        )

    v_cols[:, pl.ds(head_dim, 16)] = jnp.ones_like(v_cols[:, pl.ds(head_dim, 16)])
    group = 16
    lane = lax.broadcasted_iota(jnp.int32, (group, 128), 1)
    agg_query = query_ref[...]

    def pool(c):
        @pl.loop(0, part_rows // group)
        def _(i):
            at = pl.ds(pl.multiple_of(c * part_rows + i * group, group), group)
            logits = []
            for v in range(var_count):
                embedded = tokens[v, at].astype(jnp.float32) + embed_ref[pl.ds(v, 1)]
                logits.append(
                    jnp.sum(embedded * agg_query, -1, keepdims=True) * (1.0 / math.sqrt(D))
                )
            top = functools.reduce(jnp.maximum, logits)
            total, weighted = None, None
            for v in range(var_count):
                embedded = tokens[v, at].astype(jnp.float32) + embed_ref[pl.ds(v, 1)]
                weight = jnp.exp(logits[v] - top)
                total = weight if v == 0 else total + weight
                weighted = weight * embedded if v == 0 else weighted + weight * embedded
            acc[at] = weighted
            acc_out[at] = weighted.astype(jnp.bfloat16)
            resid_ref[at, pl.ds(0, 128)] = jnp.where(lane == 0, top, total)

    for c in range(PARTS):
        loads[c].wait()
        pool(c)
        if c == 0:
            pl.semaphore_wait(barrier, count + 1)
        for turn in range(1, chans):
            acc_copy(c, turn).start()
        if c % (PARTS // 2) == PARTS // 2 - 1:
            h = c // (PARTS // 2)
            stat[h] = resid_ref[lanes_of(h), pl.ds(0, 128)].T
            for turn in range(1, chans):
                stat_copy(h, turn).start()

    def take(slot, h, keys, values):
        k_rows[slot, lanes_of(h)] = keys.T
        v_cols[slot, pl.ds(0, head_dim), lanes_of(h)] = values

    load_pos.wait()
    gain = gain_ref[...]
    spread = 128
    for h in range(2):
        for slot in range(chans - 1):
            stat_copy(h, chans - 1 - slot).wait_recv()
            for c in range(h * PARTS // 2, (h + 1) * PARTS // 2):
                acc_copy(c, chans - 1 - slot).wait_recv()

        for slot in range(chans - 1):
            stat_ref = stat_in.at[h, slot]
            wide = jnp.concatenate([stat_ref[...]] * (spread // 8), 0).T
            acc_stat[slot] = wide

        @pl.loop(0, half_rows // group)
        def _(i):
            near = pl.ds(pl.multiple_of(i * group, group), group)
            at = pl.ds(pl.multiple_of(h * half_rows + i * group, group), group)
            own = resid_ref[at, pl.ds(0, 128)]
            tops, totals = [own[:, 0:1]], [own[:, 1:2]]
            for slot in range(chans - 1):
                other = acc_stat[slot, near]
                tops.append(other[:, 0:1])
                totals.append(other[:, 1:2])
            top = functools.reduce(jnp.maximum, tops)
            factors = [jnp.exp(t - top) for t in tops]
            denom = functools.reduce(jnp.add, [f * t for f, t in zip(factors, totals)])
            pooled = acc[at] * (factors[0] / denom)
            for slot in range(chans - 1):
                pooled += acc_in[slot, at].astype(jnp.float32) * (factors[slot + 1] / denom)
            resid = pooled + pos[at].astype(jnp.float32)
            resid_ref[at] = resid
            normed[near] = rms_norm(resid, gain).astype(jnp.bfloat16)

        if h == 0:
            load_w.wait()
        for j in range(3):
            out = lax.dot_general(
                w_qkv[pl.ds(j * columns, columns)], normed[...], (((1,), (1,)), ((), ())),
                preferred_element_type=jnp.float32,
            )
            if j == 0:
                out = out * (math.log2(math.e) / math.sqrt(head_dim))
            qkv_ref[j, :, :, lanes_of(h)] = (
                out.astype(jnp.bfloat16).reshape(heads, head_dim, half_rows)
            )
        for step in range(1, heads):
            block_out(h, step).start()
        got[chip, :, :, lanes_of(h)] = qkv_ref[:, chip, :, lanes_of(h)]
        forward(h, chip).start()
        take(chip, h, got[chip, 1, :, lanes_of(h)], got[chip, 2, :, lanes_of(h)])

    for turn in range(1, chans):
        w_out_copy(turn).start()

    for h in range(2):
        @pl.loop(1, heads)
        def _(step):
            origin = lax.rem(chip + heads - step, heads)
            block_in(h, origin).wait_recv()
            forward(h, origin).start()
            take(origin, h, got[origin, 1, :, lanes_of(h)], got[origin, 2, :, lanes_of(h)])

    for h in range(2):
        @pl.loop(0, heads)
        def _(step):
            origin = lax.rem(chip + heads - step, heads)
            forward(h, origin).wait_recv()
            take(
                heads + origin, h, part[origin, 0, :, lanes_of(h)], part[origin, 1, :, lanes_of(h)]
            )

    blocks = 2 * heads

    def out_copy(step, turn):
        return pltpu.make_async_remote_copy(
            src_ref=stage.at[step], dst_ref=mixed_ref.at[(chans - turn) % chans, chip],
            send_sem=out_send.at[step, turn], recv_sem=out_recv.at[(chans - turn) % chans, chip],
            device_id={"space": same_core(step) * 2 + core, "chan": lax.rem(chan + turn, chans)},
            device_id_type=MESH,
        )

    def out_wait(shift, origin):
        return pltpu.make_async_remote_copy(
            src_ref=stage.at[0], dst_ref=mixed_ref.at[shift, origin],
            send_sem=out_send.at[0, 0], recv_sem=out_recv.at[shift, origin],
            device_id={"space": partner}, device_id_type=MESH,
        )

    def first_pass(step, scores):
        query = got[same_core(step), 0]

        def one(t, top):
            s = jnp.dot(k_rows[t], query, preferred_element_type=jnp.float32)
            scores[t] = s
            s_top = jnp.max(s.reshape(rows // 8, 8, rows), 0)
            return s_top if top is None else jnp.maximum(top, s_top)

        return one

    def second_pass(scores, top):
        def one(t, acc):
            p = jnp.exp2(scores[t] - top).astype(jnp.bfloat16)
            term = jnp.dot(v_cols[t], p, preferred_element_type=jnp.float32)
            return term if acc is None else acc + term

        return one

    def both(step, scores_now, top_now, scores_next):
        one_next = first_pass(step + 1, scores_next)
        one_now = second_pass(scores_now, top_now)
        top, acc = None, None
        for t in range(blocks):
            top = one_next(t, top)
            acc = one_now(t, acc)
        result = (acc[:head_dim] * (1.0 / acc[head_dim : head_dim + 1])).astype(jnp.bfloat16)
        stage[step] = result

        @pl.when(step == 0)
        def _():
            mixed_ref[0, chip] = result

        @pl.when(step != 0)
        def _():
            out_copy(step, 0).start()

        for turn in range(1, chans):
            out_copy(step, turn).start()
        return jnp.max(top, 0, keepdims=True)

    one = first_pass(0, score_a)
    top = None
    for t in range(blocks):
        top = one(t, top)
    top = jnp.max(top, 0, keepdims=True)

    def pair(i, top):
        top = both(2 * i, score_a, top, score_b)
        return both(2 * i + 1, score_b, top, score_a)

    top = lax.fori_loop(0, heads // 4, pair, top)
    for slot in range(chans - 1):
        w_out_copy(chans - 1 - slot).wait_recv()
        w_forward(slot, core).start()
    lax.fori_loop(heads // 4, heads // 2, pair, top)

    for step in range(1, heads):
        for h in range(2):
            block_out(h, step).wait_send()
        out_copy(step, 0).wait_send()
        out_wait(0, same_core(step)).wait_recv()
    for step in range(heads):
        for h in range(2):
            forward(h, step).wait_send()
        for turn in range(1, chans):
            out_copy(step, turn).wait_send()
            out_wait(turn, step).wait_recv()
    for slot in range(chans - 1):
        w_out_copy(slot + 1).wait_send()
        w_forward(slot, core).wait_send()
        w_forward(slot, 1 - core).wait_recv()
        for c in range(PARTS):
            acc_copy(c, slot + 1).wait_send()
        for h in range(2):
            stat_copy(h, slot + 1).wait_send()


def fused(patches, var_embed, agg_query, pos_embed, gain_first, w_qkv, w_out, chans):
    var_count, rows, d_model = patches.shape
    columns = w_qkv.shape[0] // 3
    head_dim = D // HEADS
    heads = columns // head_dim
    dma = pltpu.SemaphoreType.DMA
    vmem = pl.BlockSpec(memory_space=pltpu.VMEM)
    hbm = pl.BlockSpec(memory_space=pl.ANY)
    bf16, f32 = jnp.bfloat16, jnp.float32
    return pl.pallas_call(
        functools.partial(fused_kernel, chans, heads),
        out_shape=(
            jax.ShapeDtypeStruct((chans, heads, head_dim, rows), bf16),
            jax.ShapeDtypeStruct((chans - 1,) + w_out.shape, bf16),
            jax.ShapeDtypeStruct((rows, d_model), f32),
        ),
        in_specs=[hbm, vmem, vmem, hbm, vmem, hbm, hbm],
        out_specs=(vmem, hbm, vmem),
        scratch_shapes=[
            pltpu.VMEM(patches.shape, bf16),
            pltpu.VMEM(w_qkv.shape, bf16),
            pltpu.VMEM((rows, d_model), bf16),
            pltpu.VMEM((rows, d_model), f32),
            pltpu.VMEM((rows, d_model), bf16),
            pltpu.VMEM((chans - 1, rows, d_model), bf16),
            pltpu.VMEM((2, 128, rows // 2), f32),
            pltpu.VMEM((2, chans - 1, 8, rows // 2), f32),
            pltpu.VMEM((chans - 1, rows // 2, 128), f32),
            pltpu.VMEM((rows // 2, d_model), bf16),
            pltpu.VMEM((3, heads, head_dim, rows), bf16),
            pltpu.VMEM((heads, 3, head_dim, rows), bf16),
            pltpu.VMEM((heads, 2, head_dim, rows), bf16),
            pltpu.VMEM((2 * heads, rows, head_dim), bf16),
            pltpu.VMEM((2 * heads, head_dim + 16, rows), bf16),
            pltpu.VMEM((2 * heads, rows, rows), f32),
            pltpu.VMEM((2 * heads, rows, rows), f32),
            pltpu.VMEM((heads, head_dim, rows), bf16),
            dma((PARTS + 2,)),
            dma((PARTS, chans - 1)), dma((PARTS, chans - 1)),
            dma((2, chans - 1)), dma((2, chans - 1)),
            dma((2, heads)), dma((2, heads)), dma((2, heads)), dma((2, heads)),
            dma((heads, chans)), dma((chans, heads)),
            dma((chans - 1,)), dma((chans - 1,)), dma((chans - 1,)), dma((chans - 1,)),
        ],
        compiler_params=pltpu.CompilerParams(
            collective_id=0, has_side_effects=True, vmem_limit_bytes=56 * 1024 * 1024
        ),
    )(patches, var_embed, agg_query[None], pos_embed, gain_first[None], w_qkv, w_out)


def body_exchange(
    patches,
    var_embed,
    agg_query,
    pos_embed,
    gain_first,
    gain_second,
    w_qkv,
    w_out,
    w_dec,
    mod_scale,
    mod_shift,
):
    var_count, pos_rows, d_model = patches.shape
    chans = lax.axis_size("chan")
    columns = w_qkv.shape[2]
    mixed, w_more, resid = fused(
        patches, var_embed, agg_query, pos_embed, gain_first,
        w_qkv.transpose(1, 2, 0).reshape(3 * columns, d_model), w_out, chans,
    )
    mixed = mixed.reshape(chans, columns, pos_rows)
    trunk = resid
    for shift in range(chans):
        trunk = trunk + lax.dot_general(
            mixed[shift], w_out if shift == 0 else w_more[shift - 1], (((0,), (0,)), ((), ())),
            preferred_element_type=jnp.float32,
        )
    normed_two = rms_norm(trunk, gain_second).astype(jnp.bfloat16)
    modulated = (
        normed_two.astype(jnp.float32)[None] * (1.0 + mod_scale[:, None, :]) + mod_shift[:, None, :]
    ).astype(jnp.bfloat16)
    decoded = jnp.dot(
        modulated.reshape(var_count * pos_rows, d_model), w_dec, preferred_element_type=jnp.float32
    )
    return decoded.reshape(var_count, pos_rows, d_model).astype(jnp.bfloat16)


def solution(mesh):
    placed = (
        P("chan", "space", None),
        P("chan", None),
        P(),
        P("space", None),
        P(),
        P(),
        P(None, None, "chan"),
        P("chan", None),
        P(),
        P("chan", None),
        P("chan", None),
    )
    per_chan = HEADS // mesh.shape["chan"]
    body = body_exchange if mesh.shape["space"] == 2 * per_chan else body_gather
    return jax.shard_map(
        body, mesh=mesh, in_specs=placed, out_specs=P("chan", "space", None), check_vma=False
    )
```

```python
import functools
import math

import jax
import jax.numpy as jnp
from jax import lax
from jax.experimental import pallas as pl
from jax.experimental.pallas import tpu as pltpu
from jax.sharding import PartitionSpec as P

D = 1024
HEADS = 16


epsilon = 1e-06


def merged(array, axis, combine):
    everything = jax.tree.map(
        lambda part, kind: lax.all_gather(part.astype(kind), axis),
        array,
        (jnp.bfloat16, jnp.bfloat16, jnp.bfloat16),
    )

    def take(k):
        return jax.tree.map(lambda part, own: part[k].astype(own.dtype), everything, array)

    return lax.fori_loop(
        1, lax.axis_size(axis), lambda k, so_far: combine(so_far, take(k)), take(0)
    )


def rms_norm(values, gain_vec):
    return values * lax.rsqrt(jnp.mean(values * values, -1, keepdims=True) + epsilon) * gain_vec


def pool_combine(first, second):
    max_one, sum_one, acc_one = first
    max_two, sum_two, acc_two = second
    top_value = jnp.maximum(max_one, max_two)
    left_factor = jnp.exp(max_one - top_value)
    right_factor = jnp.exp(max_two - top_value)
    return (
        top_value,
        sum_one * left_factor + sum_two * right_factor,
        acc_one * left_factor[:, None] + acc_two * right_factor[:, None],
    )


def body_gather(
    patches,
    var_embed,
    agg_query,
    pos_embed,
    gain_first,
    gain_second,
    w_qkv,
    w_out,
    w_dec,
    mod_scale,
    mod_shift,
):
    var_count = patches.shape[0]
    pos_rows = patches.shape[1]
    d_model = patches.shape[2]
    share_cols = d_model // lax.axis_size("chan")
    start_col = lax.axis_index("chan") * share_cols
    embedded = patches.astype(jnp.float32) + var_embed[:, None, :]
    logits = jnp.sum(embedded * agg_query, -1) * (1.0 / math.sqrt(D))
    local_top = jnp.max(logits, 0)
    expo_terms = jnp.exp(logits - local_top)
    part_sum = jnp.sum(expo_terms, 0)
    part_acc = jnp.sum(expo_terms[:, :, None] * embedded, 0)
    _, denom_sum, pooled_acc = merged((local_top, part_sum, part_acc), "chan", pool_combine)
    resid = pooled_acc / denom_sum[:, None] + pos_embed.astype(jnp.float32)
    normed = rms_norm(resid, gain_first).astype(jnp.bfloat16)
    columns = w_qkv.shape[2]
    qkv_all = jnp.dot(
        normed, w_qkv.reshape(d_model, 3 * columns), preferred_element_type=jnp.float32
    ).astype(jnp.bfloat16)
    head_dim = D // HEADS
    head_count = columns // head_dim
    queries = qkv_all[:, :columns].reshape(pos_rows, head_count, head_dim)
    keys_mine = qkv_all[:, columns : 2 * columns]
    values_mine = qkv_all[:, 2 * columns :]
    inv_scale = 1.0 / math.sqrt(head_dim)

    def attend_block(carry, key_block, value_block):
        run_max, run_sum, run_acc = carry
        scores = (
            jnp.einsum("phd,rhd->hpr", queries, key_block, preferred_element_type=jnp.float32)
            * inv_scale
        )
        new_max = jnp.maximum(run_max, jnp.max(scores, -1))
        rescale = jnp.exp(run_max - new_max)
        weights = jnp.exp(scores - new_max[..., None])
        run_sum = run_sum * rescale + jnp.sum(weights, -1)
        run_acc = run_acc * rescale[..., None] + jnp.einsum(
            "hpr,rhd->hpd",
            weights.astype(jnp.bfloat16),
            value_block,
            preferred_element_type=jnp.float32,
        )
        return (new_max, run_sum, run_acc)

    start_state = (
        jnp.full((head_count, pos_rows), -1e30, jnp.float32),
        jnp.zeros((head_count, pos_rows), jnp.float32),
        jnp.zeros((head_count, pos_rows, head_dim), jnp.float32),
    )
    key_piece = lax.all_gather(keys_mine, "space", axis=0, tiled=True)
    value_piece = lax.all_gather(values_mine, "space", axis=0, tiled=True)
    count_rows = key_piece.shape[0]
    key_heads = key_piece.reshape(count_rows, head_count, head_dim)
    value_heads = value_piece.reshape(count_rows, head_count, head_dim)
    blocks = count_rows // 1024
    key_stack = key_heads.reshape(blocks, 1024, head_count, head_dim)
    value_stack = value_heads.reshape(blocks, 1024, head_count, head_dim)

    def step_block(state, pair_in):
        return (attend_block(state, pair_in[0], pair_in[1]), None)

    result, _ = lax.scan(step_block, start_state, (key_stack, value_stack))
    run_max, run_sum, run_acc = result
    mixed = (
        (run_acc / run_sum[..., None])
        .transpose(1, 0, 2)
        .reshape(pos_rows, columns)
        .astype(jnp.bfloat16)
    )
    partial_out = jnp.dot(mixed, w_out, preferred_element_type=jnp.float32)
    share = lax.psum_scatter(
        partial_out.astype(jnp.bfloat16), "chan", scatter_dimension=1, tiled=True
    ).astype(jnp.float32)
    trunk_part = lax.dynamic_slice_in_dim(resid, start_col, share_cols, 1) + share
    square_sum = lax.psum(jnp.sum(trunk_part * trunk_part, 1), "chan")
    gain_part = lax.dynamic_slice_in_dim(gain_second, start_col, share_cols, 0)
    normed_part = (
        trunk_part * lax.rsqrt(square_sum[:, None] / d_model + epsilon) * gain_part
    ).astype(jnp.bfloat16)
    normed_two = lax.all_gather(normed_part, "chan", axis=1, tiled=True)
    modulated = (
        normed_two.astype(jnp.float32)[None] * (1.0 + mod_scale[:, None, :]) + mod_shift[:, None, :]
    ).astype(jnp.bfloat16)
    decoded = jnp.dot(
        modulated.reshape(var_count * pos_rows, d_model), w_dec, preferred_element_type=jnp.float32
    )
    return decoded.reshape(var_count, pos_rows, d_model).astype(jnp.bfloat16)


MESH = pl.DeviceIdType.MESH
PARTS = 4


def fused_kernel(
    chans, heads,
    patches_ref, embed_ref, query_ref, pos_ref, gain_ref, w_qkv_ref, w_ref,
    mixed_ref, w_more_ref, resid_ref,
    tokens, w_qkv, pos, acc, acc_out, acc_in, stat, stat_in, acc_stat, normed, qkv_ref,
    got, part, k_rows, v_cols, score_a, score_b, stage,
    load_sem, acc_send, acc_recv, stat_send, stat_recv,
    send_sem, recv_sem, fwd_send, fwd_recv, out_send, out_recv,
    w_send, w_recv, w_fsend, w_frecv, pass_send,
):
    space = lax.axis_index("space")
    chan = lax.axis_index("chan")
    chip = space // 2
    core = space % 2
    partner = chip * 2 + (1 - core)
    var_count, rows, d_model = tokens.shape
    head_dim = qkv_ref.shape[2]
    columns = heads * head_dim
    half = w_ref.shape[0] // 2
    part_rows = rows // PARTS
    half_rows = rows // 2

    def same_core(step):
        return lax.rem(chip + step, heads)

    loads = [
        pltpu.make_async_copy(
            patches_ref.at[:, pl.ds(c * part_rows, part_rows)],
            tokens.at[:, pl.ds(c * part_rows, part_rows)], load_sem.at[c],
        )
        for c in range(PARTS)
    ]
    load_w = pltpu.make_async_copy(w_qkv_ref, w_qkv, load_sem.at[PARTS])
    load_pos = pltpu.make_async_copy(pos_ref, pos, load_sem.at[PARTS + 1])
    for copy in loads + [load_pos, load_w]:
        copy.start()

    barrier = pltpu.get_barrier_semaphore()
    count = 0
    for step in range(heads):
        for turn in range(chans):
            if (step == 0) == (turn == 0):
                continue
            pl.semaphore_signal(
                barrier, inc=1,
                device_id={"space": same_core(step) * 2 + core, "chan": lax.rem(chan + turn, chans)},
                device_id_type=MESH,
            )
            count += 1
    pl.semaphore_signal(barrier, inc=1, device_id={"space": partner}, device_id_type=MESH)

    def acc_copy(c, turn):
        place = pl.ds(c * part_rows, part_rows)
        return pltpu.make_async_remote_copy(
            src_ref=acc_out.at[place], dst_ref=acc_in.at[chans - turn - 1, place],
            send_sem=acc_send.at[c, turn - 1], recv_sem=acc_recv.at[c, chans - turn - 1],
            device_id={"chan": lax.rem(chan + turn, chans)}, device_id_type=MESH,
        )

    def stat_copy(h, turn):
        return pltpu.make_async_remote_copy(
            src_ref=stat.at[h, pl.ds(0, 8)], dst_ref=stat_in.at[h, chans - turn - 1],
            send_sem=stat_send.at[h, turn - 1], recv_sem=stat_recv.at[h, chans - turn - 1],
            device_id={"chan": lax.rem(chan + turn, chans)}, device_id_type=MESH,
        )

    def lanes_of(h):
        return pl.ds(h * half_rows, half_rows)

    def block_out(h, step):
        to = same_core(step)
        return pltpu.make_async_remote_copy(
            src_ref=qkv_ref.at[:, to, :, lanes_of(h)], dst_ref=got.at[chip, :, :, lanes_of(h)],
            send_sem=send_sem.at[h, step], recv_sem=recv_sem.at[h, chip],
            device_id={"space": to * 2 + core}, device_id_type=MESH,
        )

    def block_in(h, origin):
        return pltpu.make_async_remote_copy(
            src_ref=qkv_ref.at[:, chip, :, lanes_of(h)], dst_ref=got.at[origin, :, :, lanes_of(h)],
            send_sem=send_sem.at[h, 0], recv_sem=recv_sem.at[h, origin],
            device_id={"space": partner}, device_id_type=MESH,
        )

    def forward(h, origin):
        return pltpu.make_async_remote_copy(
            src_ref=got.at[origin, pl.ds(1, 2), :, lanes_of(h)],
            dst_ref=part.at[origin, :, :, lanes_of(h)],
            send_sem=fwd_send.at[h, origin], recv_sem=fwd_recv.at[h, origin],
            device_id={"space": partner}, device_id_type=MESH,
        )

    def w_out_copy(turn):
        return pltpu.make_async_remote_copy(
            src_ref=w_ref.at[pl.ds(core * half, half)],
            dst_ref=w_more_ref.at[chans - turn - 1, pl.ds(core * half, half)],
            send_sem=w_send.at[turn - 1], recv_sem=w_recv.at[chans - turn - 1],
            device_id={"chan": lax.rem(chan + turn, chans)}, device_id_type=MESH,
        )

    def w_forward(slot, which):
        return pltpu.make_async_remote_copy(
            src_ref=w_more_ref.at[slot, pl.ds(which * half, half)],
            dst_ref=w_more_ref.at[slot, pl.ds(which * half, half)],
            send_sem=w_fsend.at[slot], recv_sem=w_frecv.at[slot],
            device_id={"space": partner}, device_id_type=MESH,
        )

    v_cols[:, pl.ds(head_dim, 16)] = jnp.ones_like(v_cols[:, pl.ds(head_dim, 16)])
    group = 16
    lane = lax.broadcasted_iota(jnp.int32, (group, 128), 1)
    agg_query = query_ref[...]

    def pool(c):
        @pl.loop(0, part_rows // group)
        def _(i):
            at = pl.ds(pl.multiple_of(c * part_rows + i * group, group), group)
            logits = []
            for v in range(var_count):
                embedded = tokens[v, at].astype(jnp.float32) + embed_ref[pl.ds(v, 1)]
                logits.append(
                    jnp.sum(embedded * agg_query, -1, keepdims=True) * (1.0 / math.sqrt(D))
                )
            top = functools.reduce(jnp.maximum, logits)
            total, weighted = None, None
            for v in range(var_count):
                embedded = tokens[v, at].astype(jnp.float32) + embed_ref[pl.ds(v, 1)]
                weight = jnp.exp(logits[v] - top)
                total = weight if v == 0 else total + weight
                weighted = weight * embedded if v == 0 else weighted + weight * embedded
            acc[at] = weighted
            acc_out[at] = weighted.astype(jnp.bfloat16)
            resid_ref[at, pl.ds(0, 128)] = jnp.where(lane == 0, top, total)

    for c in range(PARTS):
        loads[c].wait()
        pool(c)
        if c == 0:
            pl.semaphore_wait(barrier, count + 1)
        for turn in range(1, chans):
            acc_copy(c, turn).start()
        if c % (PARTS // 2) == PARTS // 2 - 1:
            h = c // (PARTS // 2)
            stat[h] = resid_ref[lanes_of(h), pl.ds(0, 128)].T
            for turn in range(1, chans):
                stat_copy(h, turn).start()

    def take(slot, h, keys, values):
        k_rows[slot, lanes_of(h)] = keys.T
        v_cols[slot, pl.ds(0, head_dim), lanes_of(h)] = values

    load_pos.wait()
    gain = gain_ref[...]
    spread = 128
    for h in range(2):
        for slot in range(chans - 1):
            stat_copy(h, chans - 1 - slot).wait_recv()
            for c in range(h * PARTS // 2, (h + 1) * PARTS // 2):
                acc_copy(c, chans - 1 - slot).wait_recv()

        for slot in range(chans - 1):
            stat_ref = stat_in.at[h, slot]
            wide = jnp.concatenate([stat_ref[...]] * (spread // 8), 0).T
            acc_stat[slot] = wide

        @pl.loop(0, half_rows // group)
        def _(i):
            near = pl.ds(pl.multiple_of(i * group, group), group)
            at = pl.ds(pl.multiple_of(h * half_rows + i * group, group), group)
            own = resid_ref[at, pl.ds(0, 128)]
            tops, totals = [own[:, 0:1]], [own[:, 1:2]]
            for slot in range(chans - 1):
                other = acc_stat[slot, near]
                tops.append(other[:, 0:1])
                totals.append(other[:, 1:2])
            top = functools.reduce(jnp.maximum, tops)
            factors = [jnp.exp(t - top) for t in tops]
            denom = functools.reduce(jnp.add, [f * t for f, t in zip(factors, totals)])
            pooled = acc[at] * (factors[0] / denom)
            for slot in range(chans - 1):
                pooled += acc_in[slot, at].astype(jnp.float32) * (factors[slot + 1] / denom)
            resid = pooled + pos[at].astype(jnp.float32)
            resid_ref[at] = resid
            normed[near] = rms_norm(resid, gain).astype(jnp.bfloat16)

        if h == 0:
            load_w.wait()
        for j in range(3):
            out = lax.dot_general(
                w_qkv[pl.ds(j * columns, columns)], normed[...], (((1,), (1,)), ((), ())),
                preferred_element_type=jnp.float32,
            )
            if j == 0:
                out = out * (math.log2(math.e) / math.sqrt(head_dim))
            qkv_ref[j, :, :, lanes_of(h)] = (
                out.astype(jnp.bfloat16).reshape(heads, head_dim, half_rows)
            )
        for step in range(1, heads):
            block_out(h, step).start()
        got[chip, :, :, lanes_of(h)] = qkv_ref[:, chip, :, lanes_of(h)]
        forward(h, chip).start()
        take(chip, h, got[chip, 1, :, lanes_of(h)], got[chip, 2, :, lanes_of(h)])

    for turn in range(1, chans):
        w_out_copy(turn).start()

    for h in range(2):
        @pl.loop(1, heads)
        def _(step):
            origin = lax.rem(chip + heads - step, heads)
            block_in(h, origin).wait_recv()
            forward(h, origin).start()
            take(origin, h, got[origin, 1, :, lanes_of(h)], got[origin, 2, :, lanes_of(h)])

    for h in range(2):
        @pl.loop(0, heads)
        def _(step):
            origin = lax.rem(chip + heads - step, heads)
            forward(h, origin).wait_recv()
            take(
                heads + origin, h, part[origin, 0, :, lanes_of(h)], part[origin, 1, :, lanes_of(h)]
            )

    blocks = 2 * heads

    def out_copy(step, turn):
        return pltpu.make_async_remote_copy(
            src_ref=stage.at[step], dst_ref=mixed_ref.at[(chans - turn) % chans, chip],
            send_sem=out_send.at[step, turn], recv_sem=out_recv.at[(chans - turn) % chans, chip],
            device_id={"space": same_core(step) * 2 + core, "chan": lax.rem(chan + turn, chans)},
            device_id_type=MESH,
        )

    def out_wait(shift, origin):
        return pltpu.make_async_remote_copy(
            src_ref=stage.at[0], dst_ref=mixed_ref.at[shift, origin],
            send_sem=out_send.at[0, 0], recv_sem=out_recv.at[shift, origin],
            device_id={"space": partner}, device_id_type=MESH,
        )

    def pass_on(origin, turn):
        return pltpu.make_async_remote_copy(
            src_ref=mixed_ref.at[0, origin], dst_ref=mixed_ref.at[(chans - turn) % chans, origin],
            send_sem=pass_send.at[origin, turn - 1],
            recv_sem=out_recv.at[(chans - turn) % chans, origin],
            device_id={"chan": lax.rem(chan + turn, chans)}, device_id_type=MESH,
        )

    def relay(step):
        origin = lax.rem(chip + heads - step, heads)
        out_wait(0, origin).wait_recv()
        for turn in range(1, chans):
            pass_on(origin, turn).start()

    def first_pass(step, scores):
        query = got[same_core(step), 0]

        def one(t, top):
            s = jnp.dot(k_rows[t], query, preferred_element_type=jnp.float32)
            scores[t] = s
            s_top = jnp.max(s.reshape(rows // 8, 8, rows), 0)
            return s_top if top is None else jnp.maximum(top, s_top)

        return one

    def second_pass(scores, top):
        def one(t, acc):
            p = jnp.exp2(scores[t] - top).astype(jnp.bfloat16)
            term = jnp.dot(v_cols[t], p, preferred_element_type=jnp.float32)
            return term if acc is None else acc + term

        return one

    def both(step, scores_now, top_now, scores_next):
        one_next = first_pass(step + 1, scores_next)
        one_now = second_pass(scores_now, top_now)
        top, acc = None, None
        for t in range(blocks):
            top = one_next(t, top)
            acc = one_now(t, acc)
        result = (acc[:head_dim] * (1.0 / acc[head_dim : head_dim + 1])).astype(jnp.bfloat16)
        stage[step] = result

        @pl.when(step == 0)
        def _():
            mixed_ref[0, chip] = result
            for turn in range(1, chans):
                out_copy(step, turn).start()

        @pl.when(step != 0)
        def _():
            out_copy(step, 0).start()

        return jnp.max(top, 0, keepdims=True)

    one = first_pass(0, score_a)
    top = None
    for t in range(blocks):
        top = one(t, top)
    top = jnp.max(top, 0, keepdims=True)

    def pair(i, top):
        top = both(2 * i, score_a, top, score_b)
        top = both(2 * i + 1, score_b, top, score_a)

        @pl.when(i > 1)
        def _():
            relay(2 * i - 2)

        @pl.when(i > 0)
        def _():
            relay(2 * i - 1)

        return top

    top = lax.fori_loop(0, heads // 4, pair, top)
    for slot in range(chans - 1):
        w_out_copy(chans - 1 - slot).wait_recv()
        w_forward(slot, core).start()
    lax.fori_loop(heads // 4, heads // 2, pair, top)

    for step in range(heads - 2, heads):
        relay(step)
    for step in range(1, heads):
        for h in range(2):
            block_out(h, step).wait_send()
        out_copy(step, 0).wait_send()
    for step in range(heads):
        for h in range(2):
            forward(h, step).wait_send()
        for turn in range(1, chans):
            if step == 0:
                out_copy(step, turn).wait_send()
            else:
                pass_on(same_core(step), turn).wait_send()
            out_wait(turn, step).wait_recv()
    for slot in range(chans - 1):
        w_out_copy(slot + 1).wait_send()
        w_forward(slot, core).wait_send()
        w_forward(slot, 1 - core).wait_recv()
        for c in range(PARTS):
            acc_copy(c, slot + 1).wait_send()
        for h in range(2):
            stat_copy(h, slot + 1).wait_send()


def fused(patches, var_embed, agg_query, pos_embed, gain_first, w_qkv, w_out, chans):
    var_count, rows, d_model = patches.shape
    columns = w_qkv.shape[0] // 3
    head_dim = D // HEADS
    heads = columns // head_dim
    dma = pltpu.SemaphoreType.DMA
    vmem = pl.BlockSpec(memory_space=pltpu.VMEM)
    hbm = pl.BlockSpec(memory_space=pl.ANY)
    bf16, f32 = jnp.bfloat16, jnp.float32
    return pl.pallas_call(
        functools.partial(fused_kernel, chans, heads),
        out_shape=(
            jax.ShapeDtypeStruct((chans, heads, head_dim, rows), bf16),
            jax.ShapeDtypeStruct((chans - 1,) + w_out.shape, bf16),
            jax.ShapeDtypeStruct((rows, d_model), f32),
        ),
        in_specs=[hbm, vmem, vmem, hbm, vmem, hbm, hbm],
        out_specs=(vmem, hbm, vmem),
        scratch_shapes=[
            pltpu.VMEM(patches.shape, bf16),
            pltpu.VMEM(w_qkv.shape, bf16),
            pltpu.VMEM((rows, d_model), bf16),
            pltpu.VMEM((rows, d_model), f32),
            pltpu.VMEM((rows, d_model), bf16),
            pltpu.VMEM((chans - 1, rows, d_model), bf16),
            pltpu.VMEM((2, 128, rows // 2), f32),
            pltpu.VMEM((2, chans - 1, 8, rows // 2), f32),
            pltpu.VMEM((chans - 1, rows // 2, 128), f32),
            pltpu.VMEM((rows // 2, d_model), bf16),
            pltpu.VMEM((3, heads, head_dim, rows), bf16),
            pltpu.VMEM((heads, 3, head_dim, rows), bf16),
            pltpu.VMEM((heads, 2, head_dim, rows), bf16),
            pltpu.VMEM((2 * heads, rows, head_dim), bf16),
            pltpu.VMEM((2 * heads, head_dim + 16, rows), bf16),
            pltpu.VMEM((2 * heads, rows, rows), f32),
            pltpu.VMEM((2 * heads, rows, rows), f32),
            pltpu.VMEM((heads, head_dim, rows), bf16),
            dma((PARTS + 2,)),
            dma((PARTS, chans - 1)), dma((PARTS, chans - 1)),
            dma((2, chans - 1)), dma((2, chans - 1)),
            dma((2, heads)), dma((2, heads)), dma((2, heads)), dma((2, heads)),
            dma((heads, chans)), dma((chans, heads)),
            dma((chans - 1,)), dma((chans - 1,)), dma((chans - 1,)), dma((chans - 1,)),
            dma((heads, chans - 1)),
        ],
        compiler_params=pltpu.CompilerParams(
            collective_id=0, has_side_effects=True, vmem_limit_bytes=56 * 1024 * 1024
        ),
    )(patches, var_embed, agg_query[None], pos_embed, gain_first[None], w_qkv, w_out)


def body_exchange(
    patches,
    var_embed,
    agg_query,
    pos_embed,
    gain_first,
    gain_second,
    w_qkv,
    w_out,
    w_dec,
    mod_scale,
    mod_shift,
):
    var_count, pos_rows, d_model = patches.shape
    chans = lax.axis_size("chan")
    columns = w_qkv.shape[2]
    mixed, w_more, resid = fused(
        patches, var_embed, agg_query, pos_embed, gain_first,
        w_qkv.transpose(1, 2, 0).reshape(3 * columns, d_model), w_out, chans,
    )
    mixed = mixed.reshape(chans, columns, pos_rows)
    trunk = resid
    for shift in range(chans):
        trunk = trunk + lax.dot_general(
            mixed[shift], w_out if shift == 0 else w_more[shift - 1], (((0,), (0,)), ((), ())),
            preferred_element_type=jnp.float32,
        )
    normed_two = rms_norm(trunk, gain_second).astype(jnp.bfloat16)
    modulated = (
        normed_two.astype(jnp.float32)[None] * (1.0 + mod_scale[:, None, :]) + mod_shift[:, None, :]
    ).astype(jnp.bfloat16)
    decoded = jnp.dot(
        modulated.reshape(var_count * pos_rows, d_model), w_dec, preferred_element_type=jnp.float32
    )
    return decoded.reshape(var_count, pos_rows, d_model).astype(jnp.bfloat16)


def solution(mesh):
    placed = (
        P("chan", "space", None),
        P("chan", None),
        P(),
        P("space", None),
        P(),
        P(),
        P(None, None, "chan"),
        P("chan", None),
        P(),
        P("chan", None),
        P("chan", None),
    )
    per_chan = HEADS // mesh.shape["chan"]
    body = body_exchange if mesh.shape["space"] == 2 * per_chan else body_gather
    return jax.shard_map(
        body, mesh=mesh, in_specs=placed, out_specs=P("chan", "space", None), check_vma=False
    )
```

```python
import functools
import math

import jax
import jax.numpy as jnp
from jax import lax
from jax.experimental import pallas as pl
from jax.experimental.pallas import tpu as pltpu
from jax.sharding import PartitionSpec as P

D = 1024
HEADS = 16


epsilon = 1e-06


def merged(array, axis, combine):
    everything = jax.tree.map(
        lambda part, kind: lax.all_gather(part.astype(kind), axis),
        array,
        (jnp.bfloat16, jnp.bfloat16, jnp.bfloat16),
    )

    def take(k):
        return jax.tree.map(lambda part, own: part[k].astype(own.dtype), everything, array)

    return lax.fori_loop(
        1, lax.axis_size(axis), lambda k, so_far: combine(so_far, take(k)), take(0)
    )


def rms_norm(values, gain_vec):
    return values * lax.rsqrt(jnp.mean(values * values, -1, keepdims=True) + epsilon) * gain_vec


def pool_combine(first, second):
    max_one, sum_one, acc_one = first
    max_two, sum_two, acc_two = second
    top_value = jnp.maximum(max_one, max_two)
    left_factor = jnp.exp(max_one - top_value)
    right_factor = jnp.exp(max_two - top_value)
    return (
        top_value,
        sum_one * left_factor + sum_two * right_factor,
        acc_one * left_factor[:, None] + acc_two * right_factor[:, None],
    )


def body_gather(
    patches,
    var_embed,
    agg_query,
    pos_embed,
    gain_first,
    gain_second,
    w_qkv,
    w_out,
    w_dec,
    mod_scale,
    mod_shift,
):
    var_count = patches.shape[0]
    pos_rows = patches.shape[1]
    d_model = patches.shape[2]
    share_cols = d_model // lax.axis_size("chan")
    start_col = lax.axis_index("chan") * share_cols
    embedded = patches.astype(jnp.float32) + var_embed[:, None, :]
    logits = jnp.sum(embedded * agg_query, -1) * (1.0 / math.sqrt(D))
    local_top = jnp.max(logits, 0)
    expo_terms = jnp.exp(logits - local_top)
    part_sum = jnp.sum(expo_terms, 0)
    part_acc = jnp.sum(expo_terms[:, :, None] * embedded, 0)
    _, denom_sum, pooled_acc = merged((local_top, part_sum, part_acc), "chan", pool_combine)
    resid = pooled_acc / denom_sum[:, None] + pos_embed.astype(jnp.float32)
    normed = rms_norm(resid, gain_first).astype(jnp.bfloat16)
    columns = w_qkv.shape[2]
    qkv_all = jnp.dot(
        normed, w_qkv.reshape(d_model, 3 * columns), preferred_element_type=jnp.float32
    ).astype(jnp.bfloat16)
    head_dim = D // HEADS
    head_count = columns // head_dim
    queries = qkv_all[:, :columns].reshape(pos_rows, head_count, head_dim)
    keys_mine = qkv_all[:, columns : 2 * columns]
    values_mine = qkv_all[:, 2 * columns :]
    inv_scale = 1.0 / math.sqrt(head_dim)

    def attend_block(carry, key_block, value_block):
        run_max, run_sum, run_acc = carry
        scores = (
            jnp.einsum("phd,rhd->hpr", queries, key_block, preferred_element_type=jnp.float32)
            * inv_scale
        )
        new_max = jnp.maximum(run_max, jnp.max(scores, -1))
        rescale = jnp.exp(run_max - new_max)
        weights = jnp.exp(scores - new_max[..., None])
        run_sum = run_sum * rescale + jnp.sum(weights, -1)
        run_acc = run_acc * rescale[..., None] + jnp.einsum(
            "hpr,rhd->hpd",
            weights.astype(jnp.bfloat16),
            value_block,
            preferred_element_type=jnp.float32,
        )
        return (new_max, run_sum, run_acc)

    start_state = (
        jnp.full((head_count, pos_rows), -1e30, jnp.float32),
        jnp.zeros((head_count, pos_rows), jnp.float32),
        jnp.zeros((head_count, pos_rows, head_dim), jnp.float32),
    )
    key_piece = lax.all_gather(keys_mine, "space", axis=0, tiled=True)
    value_piece = lax.all_gather(values_mine, "space", axis=0, tiled=True)
    count_rows = key_piece.shape[0]
    key_heads = key_piece.reshape(count_rows, head_count, head_dim)
    value_heads = value_piece.reshape(count_rows, head_count, head_dim)
    blocks = count_rows // 1024
    key_stack = key_heads.reshape(blocks, 1024, head_count, head_dim)
    value_stack = value_heads.reshape(blocks, 1024, head_count, head_dim)

    def step_block(state, pair_in):
        return (attend_block(state, pair_in[0], pair_in[1]), None)

    result, _ = lax.scan(step_block, start_state, (key_stack, value_stack))
    run_max, run_sum, run_acc = result
    mixed = (
        (run_acc / run_sum[..., None])
        .transpose(1, 0, 2)
        .reshape(pos_rows, columns)
        .astype(jnp.bfloat16)
    )
    partial_out = jnp.dot(mixed, w_out, preferred_element_type=jnp.float32)
    share = lax.psum_scatter(
        partial_out.astype(jnp.bfloat16), "chan", scatter_dimension=1, tiled=True
    ).astype(jnp.float32)
    trunk_part = lax.dynamic_slice_in_dim(resid, start_col, share_cols, 1) + share
    square_sum = lax.psum(jnp.sum(trunk_part * trunk_part, 1), "chan")
    gain_part = lax.dynamic_slice_in_dim(gain_second, start_col, share_cols, 0)
    normed_part = (
        trunk_part * lax.rsqrt(square_sum[:, None] / d_model + epsilon) * gain_part
    ).astype(jnp.bfloat16)
    normed_two = lax.all_gather(normed_part, "chan", axis=1, tiled=True)
    modulated = (
        normed_two.astype(jnp.float32)[None] * (1.0 + mod_scale[:, None, :]) + mod_shift[:, None, :]
    ).astype(jnp.bfloat16)
    decoded = jnp.dot(
        modulated.reshape(var_count * pos_rows, d_model), w_dec, preferred_element_type=jnp.float32
    )
    return decoded.reshape(var_count, pos_rows, d_model).astype(jnp.bfloat16)


MESH = pl.DeviceIdType.MESH
PARTS = 4


def fused_kernel(
    chans, heads,
    patches_ref, embed_ref, query_ref, pos_ref, gain_ref, w_qkv_ref, w_ref,
    mixed_ref, w_more_ref, resid_ref,
    tokens, w_qkv, pos, acc, acc_out, acc_in, stat, stat_in, acc_stat, normed, qkv_ref,
    got, part, k_rows, v_cols, score_a, score_b, stage,
    load_sem, acc_send, acc_recv, stat_send, stat_recv,
    send_sem, recv_sem, fwd_send, fwd_recv, out_send, out_recv,
    w_send, w_recv, w_fsend, w_frecv,
):
    space = lax.axis_index("space")
    chan = lax.axis_index("chan")
    chip = space // 2
    core = space % 2
    partner = chip * 2 + (1 - core)
    var_count, rows, d_model = tokens.shape
    head_dim = qkv_ref.shape[2]
    columns = heads * head_dim
    half = w_ref.shape[0] // 2
    part_rows = rows // PARTS
    half_rows = rows // 2

    def same_core(step):
        return lax.rem(chip + step, heads)

    loads = [
        pltpu.make_async_copy(
            patches_ref.at[:, pl.ds(c * part_rows, part_rows)],
            tokens.at[:, pl.ds(c * part_rows, part_rows)], load_sem.at[c],
        )
        for c in range(PARTS)
    ]
    load_w = pltpu.make_async_copy(w_qkv_ref, w_qkv, load_sem.at[PARTS])
    load_pos = pltpu.make_async_copy(pos_ref, pos, load_sem.at[PARTS + 1])
    for copy in loads + [load_pos, load_w]:
        copy.start()

    barrier = pltpu.get_barrier_semaphore()
    count = 0
    for step in range(heads):
        for turn in range(chans):
            if step == 0 and turn == 0:
                continue
            pl.semaphore_signal(
                barrier, inc=1,
                device_id={"space": same_core(step) * 2 + core, "chan": lax.rem(chan + turn, chans)},
                device_id_type=MESH,
            )
            count += 1
    pl.semaphore_signal(barrier, inc=1, device_id={"space": partner}, device_id_type=MESH)

    def acc_copy(c, turn):
        place = pl.ds(c * part_rows, part_rows)
        return pltpu.make_async_remote_copy(
            src_ref=acc_out.at[place], dst_ref=acc_in.at[chans - turn - 1, place],
            send_sem=acc_send.at[c, turn - 1], recv_sem=acc_recv.at[c, chans - turn - 1],
            device_id={"chan": lax.rem(chan + turn, chans)}, device_id_type=MESH,
        )

    def stat_copy(h, turn):
        return pltpu.make_async_remote_copy(
            src_ref=stat.at[h, pl.ds(0, 8)], dst_ref=stat_in.at[h, chans - turn - 1],
            send_sem=stat_send.at[h, turn - 1], recv_sem=stat_recv.at[h, chans - turn - 1],
            device_id={"chan": lax.rem(chan + turn, chans)}, device_id_type=MESH,
        )

    def lanes_of(h):
        return pl.ds(h * half_rows, half_rows)

    def block_out(h, step):
        to = same_core(step)
        return pltpu.make_async_remote_copy(
            src_ref=qkv_ref.at[:, to, :, lanes_of(h)], dst_ref=got.at[chip, :, :, lanes_of(h)],
            send_sem=send_sem.at[h, step], recv_sem=recv_sem.at[h, chip],
            device_id={"space": to * 2 + core}, device_id_type=MESH,
        )

    def block_in(h, origin):
        return pltpu.make_async_remote_copy(
            src_ref=qkv_ref.at[:, chip, :, lanes_of(h)], dst_ref=got.at[origin, :, :, lanes_of(h)],
            send_sem=send_sem.at[h, 0], recv_sem=recv_sem.at[h, origin],
            device_id={"space": partner}, device_id_type=MESH,
        )

    def forward(h, origin):
        return pltpu.make_async_remote_copy(
            src_ref=got.at[origin, pl.ds(1, 2), :, lanes_of(h)],
            dst_ref=part.at[origin, :, :, lanes_of(h)],
            send_sem=fwd_send.at[h, origin], recv_sem=fwd_recv.at[h, origin],
            device_id={"space": partner}, device_id_type=MESH,
        )

    def w_out_copy(turn):
        return pltpu.make_async_remote_copy(
            src_ref=w_ref.at[pl.ds(core * half, half)],
            dst_ref=w_more_ref.at[chans - turn - 1, pl.ds(core * half, half)],
            send_sem=w_send.at[turn - 1], recv_sem=w_recv.at[chans - turn - 1],
            device_id={"chan": lax.rem(chan + turn, chans)}, device_id_type=MESH,
        )

    def w_forward(slot, which):
        return pltpu.make_async_remote_copy(
            src_ref=w_more_ref.at[slot, pl.ds(which * half, half)],
            dst_ref=w_more_ref.at[slot, pl.ds(which * half, half)],
            send_sem=w_fsend.at[slot], recv_sem=w_frecv.at[slot],
            device_id={"space": partner}, device_id_type=MESH,
        )

    v_cols[:, pl.ds(head_dim, 16)] = jnp.ones_like(v_cols[:, pl.ds(head_dim, 16)])
    group = 16
    lane = lax.broadcasted_iota(jnp.int32, (group, 128), 1)
    agg_query = query_ref[...]

    def pool(c):
        @pl.loop(0, part_rows // group)
        def _(i):
            at = pl.ds(pl.multiple_of(c * part_rows + i * group, group), group)
            logits = []
            for v in range(var_count):
                embedded = tokens[v, at].astype(jnp.float32) + embed_ref[pl.ds(v, 1)]
                logits.append(
                    jnp.sum(embedded * agg_query, -1, keepdims=True) * (1.0 / math.sqrt(D))
                )
            top = functools.reduce(jnp.maximum, logits)
            total, weighted = None, None
            for v in range(var_count):
                embedded = tokens[v, at].astype(jnp.float32) + embed_ref[pl.ds(v, 1)]
                weight = jnp.exp(logits[v] - top)
                total = weight if v == 0 else total + weight
                weighted = weight * embedded if v == 0 else weighted + weight * embedded
            acc[at] = weighted
            acc_out[at] = weighted.astype(jnp.bfloat16)
            resid_ref[at, pl.ds(0, 128)] = jnp.where(lane == 0, top, total)

    for c in range(PARTS):
        loads[c].wait()
        pool(c)
        if c == 0:
            pl.semaphore_wait(barrier, count + 1)
        for turn in range(1, chans):
            acc_copy(c, turn).start()
        if c % (PARTS // 2) == PARTS // 2 - 1:
            h = c // (PARTS // 2)
            stat[h] = resid_ref[lanes_of(h), pl.ds(0, 128)].T
            for turn in range(1, chans):
                stat_copy(h, turn).start()

    def take(slot, h, keys, values):
        k_rows[slot, lanes_of(h)] = keys.T
        v_cols[slot, pl.ds(0, head_dim), lanes_of(h)] = values

    load_pos.wait()
    gain = gain_ref[...]
    spread = 128
    for h in range(2):
        for slot in range(chans - 1):
            stat_copy(h, chans - 1 - slot).wait_recv()
            for c in range(h * PARTS // 2, (h + 1) * PARTS // 2):
                acc_copy(c, chans - 1 - slot).wait_recv()

        for slot in range(chans - 1):
            stat_ref = stat_in.at[h, slot]
            wide = jnp.concatenate([stat_ref[...]] * (spread // 8), 0).T
            acc_stat[slot] = wide

        @pl.loop(0, half_rows // group)
        def _(i):
            near = pl.ds(pl.multiple_of(i * group, group), group)
            at = pl.ds(pl.multiple_of(h * half_rows + i * group, group), group)
            own = resid_ref[at, pl.ds(0, 128)]
            tops, totals = [own[:, 0:1]], [own[:, 1:2]]
            for slot in range(chans - 1):
                other = acc_stat[slot, near]
                tops.append(other[:, 0:1])
                totals.append(other[:, 1:2])
            top = functools.reduce(jnp.maximum, tops)
            factors = [jnp.exp(t - top) for t in tops]
            denom = functools.reduce(jnp.add, [f * t for f, t in zip(factors, totals)])
            pooled = acc[at] * (factors[0] / denom)
            for slot in range(chans - 1):
                pooled += acc_in[slot, at].astype(jnp.float32) * (factors[slot + 1] / denom)
            resid = pooled + pos[at].astype(jnp.float32)
            resid_ref[at] = resid
            normed[near] = rms_norm(resid, gain).astype(jnp.bfloat16)

        if h == 0:
            load_w.wait()
        for j in range(3):
            out = lax.dot_general(
                w_qkv[pl.ds(j * columns, columns)], normed[...], (((1,), (1,)), ((), ())),
                preferred_element_type=jnp.float32,
            )
            if j == 0:
                out = out * (math.log2(math.e) / math.sqrt(head_dim))
            qkv_ref[j, :, :, lanes_of(h)] = (
                out.astype(jnp.bfloat16).reshape(heads, head_dim, half_rows)
            )
        for step in sorted(range(1, heads), key=lambda k: -min(k, heads - k)):
            block_out(h, step).start()
        got[chip, :, :, lanes_of(h)] = qkv_ref[:, chip, :, lanes_of(h)]
        forward(h, chip).start()
        take(chip, h, got[chip, 1, :, lanes_of(h)], got[chip, 2, :, lanes_of(h)])

    for turn in range(1, chans):
        w_out_copy(turn).start()

    for h in range(2):
        for step in sorted(range(1, heads), key=lambda k: -min(k, heads - k)):
            origin = lax.rem(chip + heads - step, heads)
            block_in(h, origin).wait_recv()
            forward(h, origin).start()
            take(origin, h, got[origin, 1, :, lanes_of(h)], got[origin, 2, :, lanes_of(h)])

    for h in range(2):
        @pl.loop(0, heads)
        def _(step):
            origin = lax.rem(chip + heads - step, heads)
            forward(h, origin).wait_recv()
            take(
                heads + origin, h, part[origin, 0, :, lanes_of(h)], part[origin, 1, :, lanes_of(h)]
            )

    blocks = 2 * heads

    def out_copy(step, turn):
        return pltpu.make_async_remote_copy(
            src_ref=stage.at[step], dst_ref=mixed_ref.at[(chans - turn) % chans, chip],
            send_sem=out_send.at[step, turn], recv_sem=out_recv.at[(chans - turn) % chans, chip],
            device_id={"space": same_core(step) * 2 + core, "chan": lax.rem(chan + turn, chans)},
            device_id_type=MESH,
        )

    def out_wait(shift, origin):
        return pltpu.make_async_remote_copy(
            src_ref=stage.at[0], dst_ref=mixed_ref.at[shift, origin],
            send_sem=out_send.at[0, 0], recv_sem=out_recv.at[shift, origin],
            device_id={"space": partner}, device_id_type=MESH,
        )

    def first_pass(step, scores):
        query = got[same_core(step), 0]

        def one(t, top):
            s = jnp.dot(k_rows[t], query, preferred_element_type=jnp.float32)
            scores[t] = s
            s_top = jnp.max(s.reshape(rows // 8, 8, rows), 0)
            return s_top if top is None else jnp.maximum(top, s_top)

        return one

    def second_pass(scores, top):
        def one(t, acc):
            p = jnp.exp2(scores[t] - top).astype(jnp.bfloat16)
            term = jnp.dot(v_cols[t], p, preferred_element_type=jnp.float32)
            return term if acc is None else acc + term

        return one

    def both(step, scores_now, top_now, scores_next):
        one_next = first_pass(step + 1, scores_next)
        one_now = second_pass(scores_now, top_now)
        top, acc = None, None
        for t in range(blocks):
            top = one_next(t, top)
            acc = one_now(t, acc)
        result = (acc[:head_dim] * (1.0 / acc[head_dim : head_dim + 1])).astype(jnp.bfloat16)
        stage[step] = result

        @pl.when(step == 0)
        def _():
            mixed_ref[0, chip] = result

        @pl.when(step != 0)
        def _():
            out_copy(step, 0).start()

        for turn in range(1, chans):
            out_copy(step, turn).start()
        return jnp.max(top, 0, keepdims=True)

    one = first_pass(0, score_a)
    top = None
    for t in range(blocks):
        top = one(t, top)
    top = jnp.max(top, 0, keepdims=True)

    def pair(i, top):
        top = both(2 * i, score_a, top, score_b)
        return both(2 * i + 1, score_b, top, score_a)

    top = lax.fori_loop(0, heads // 4, pair, top)
    for slot in range(chans - 1):
        w_out_copy(chans - 1 - slot).wait_recv()
        w_forward(slot, core).start()
    lax.fori_loop(heads // 4, heads // 2, pair, top)

    for step in range(1, heads):
        for h in range(2):
            block_out(h, step).wait_send()
        out_copy(step, 0).wait_send()
        out_wait(0, same_core(step)).wait_recv()
    for step in range(heads):
        for h in range(2):
            forward(h, step).wait_send()
        for turn in range(1, chans):
            out_copy(step, turn).wait_send()
            out_wait(turn, step).wait_recv()
    for slot in range(chans - 1):
        w_out_copy(slot + 1).wait_send()
        w_forward(slot, core).wait_send()
        w_forward(slot, 1 - core).wait_recv()
        for c in range(PARTS):
            acc_copy(c, slot + 1).wait_send()
        for h in range(2):
            stat_copy(h, slot + 1).wait_send()


def fused(patches, var_embed, agg_query, pos_embed, gain_first, w_qkv, w_out, chans):
    var_count, rows, d_model = patches.shape
    columns = w_qkv.shape[0] // 3
    head_dim = D // HEADS
    heads = columns // head_dim
    dma = pltpu.SemaphoreType.DMA
    vmem = pl.BlockSpec(memory_space=pltpu.VMEM)
    hbm = pl.BlockSpec(memory_space=pl.ANY)
    bf16, f32 = jnp.bfloat16, jnp.float32
    return pl.pallas_call(
        functools.partial(fused_kernel, chans, heads),
        out_shape=(
            jax.ShapeDtypeStruct((chans, heads, head_dim, rows), bf16),
            jax.ShapeDtypeStruct((chans - 1,) + w_out.shape, bf16),
            jax.ShapeDtypeStruct((rows, d_model), f32),
        ),
        in_specs=[hbm, vmem, vmem, hbm, vmem, hbm, hbm],
        out_specs=(vmem, hbm, vmem),
        scratch_shapes=[
            pltpu.VMEM(patches.shape, bf16),
            pltpu.VMEM(w_qkv.shape, bf16),
            pltpu.VMEM((rows, d_model), bf16),
            pltpu.VMEM((rows, d_model), f32),
            pltpu.VMEM((rows, d_model), bf16),
            pltpu.VMEM((chans - 1, rows, d_model), bf16),
            pltpu.VMEM((2, 128, rows // 2), f32),
            pltpu.VMEM((2, chans - 1, 8, rows // 2), f32),
            pltpu.VMEM((chans - 1, rows // 2, 128), f32),
            pltpu.VMEM((rows // 2, d_model), bf16),
            pltpu.VMEM((3, heads, head_dim, rows), bf16),
            pltpu.VMEM((heads, 3, head_dim, rows), bf16),
            pltpu.VMEM((heads, 2, head_dim, rows), bf16),
            pltpu.VMEM((2 * heads, rows, head_dim), bf16),
            pltpu.VMEM((2 * heads, head_dim + 16, rows), bf16),
            pltpu.VMEM((2 * heads, rows, rows), f32),
            pltpu.VMEM((2 * heads, rows, rows), f32),
            pltpu.VMEM((heads, head_dim, rows), bf16),
            dma((PARTS + 2,)),
            dma((PARTS, chans - 1)), dma((PARTS, chans - 1)),
            dma((2, chans - 1)), dma((2, chans - 1)),
            dma((2, heads)), dma((2, heads)), dma((2, heads)), dma((2, heads)),
            dma((heads, chans)), dma((chans, heads)),
            dma((chans - 1,)), dma((chans - 1,)), dma((chans - 1,)), dma((chans - 1,)),
        ],
        compiler_params=pltpu.CompilerParams(
            collective_id=0, has_side_effects=True, vmem_limit_bytes=56 * 1024 * 1024
        ),
    )(patches, var_embed, agg_query[None], pos_embed, gain_first[None], w_qkv, w_out)


def body_exchange(
    patches,
    var_embed,
    agg_query,
    pos_embed,
    gain_first,
    gain_second,
    w_qkv,
    w_out,
    w_dec,
    mod_scale,
    mod_shift,
):
    var_count, pos_rows, d_model = patches.shape
    chans = lax.axis_size("chan")
    columns = w_qkv.shape[2]
    mixed, w_more, resid = fused(
        patches, var_embed, agg_query, pos_embed, gain_first,
        w_qkv.transpose(1, 2, 0).reshape(3 * columns, d_model), w_out, chans,
    )
    mixed = mixed.reshape(chans, columns, pos_rows)
    trunk = resid
    for shift in range(chans):
        trunk = trunk + lax.dot_general(
            mixed[shift], w_out if shift == 0 else w_more[shift - 1], (((0,), (0,)), ((), ())),
            preferred_element_type=jnp.float32,
        )
    normed_two = rms_norm(trunk, gain_second).astype(jnp.bfloat16)
    modulated = (
        normed_two.astype(jnp.float32)[None] * (1.0 + mod_scale[:, None, :]) + mod_shift[:, None, :]
    ).astype(jnp.bfloat16)
    decoded = jnp.dot(
        modulated.reshape(var_count * pos_rows, d_model), w_dec, preferred_element_type=jnp.float32
    )
    return decoded.reshape(var_count, pos_rows, d_model).astype(jnp.bfloat16)


def solution(mesh):
    placed = (
        P("chan", "space", None),
        P("chan", None),
        P(),
        P("space", None),
        P(),
        P(),
        P(None, None, "chan"),
        P("chan", None),
        P(),
        P("chan", None),
        P("chan", None),
    )
    per_chan = HEADS // mesh.shape["chan"]
    body = body_exchange if mesh.shape["space"] == 2 * per_chan else body_gather
    return jax.shard_map(
        body, mesh=mesh, in_specs=placed, out_specs=P("chan", "space", None), check_vma=False
    )
```
